256 devices in a mesh: tm: 8 (over y, core), space: 32 (over z, x).
Axes of the slice: x: 4, y: 4, z: 8, core: 2. Of those that a mesh axis runs over, the one named last changes fastest.
Arguments:
- background: bfloat16 [262144, 64], P('space'), may hold values from -4 to 4
- probe: bfloat16 [64, 32], replicated, may hold values from -0.75 to 0.75
- member_scale: float32 [64], replicated, may hold values from 0.5 to 2
- decay: float32 [24, 32], P('tm'), may hold values from 0.36 to 1
- inflation: float32 [24], P('tm'), may hold values from 0.05 to 0.5
- obs_owner: int32 [24, 65536, 1], P('tm', 'space'), may hold values from 0 to 31; in each aligned block of 2048 rows (0 to 2047, 2048 to 4095, ..., all dimensions but the last counted through in order) at most 128 rows name the same one
- obs_offset: int32 [24, 65536], P('tm', 'space'), may hold values from 0 to 8191
- obs_value: float32 [24, 65536], P('tm', 'space'), may hold values from -360 to 360
- obs_weight: float32 [24, 65536], P('tm', 'space'), may hold values from 0.0002 to 0.002
Outputs:
- smooth_mean: float32 [24, 262144], P('tm', 'space')
- smooth_spread: float32 [24, 262144], P('tm', 'space')
The draws below stay inside these ranges and needn't reach their ends.
Inputs may be any that keep to these rules, and one draw needn't show every extreme that they name: `obs_owner`: of the 2048 observations that one reader holds for one day, at most 128 name the same owner, and 128 is reached.
All inputs are finite; a program needn't handle non-finite values.
Results may differ from the reference program's by a relative error of at most 0.0029.
Values sent between devices are 32-bit elements; how exact they have to be, the bound alone decides.
No kernel may reach another device: no remote copies, remote signals or barrier semaphores. Data moves between devices by JAX's collectives and lax.ppermute only.
A program may use at most 64 MiB of HBM per device.

```python
import math
import jax
import jax.numpy as jnp
import numpy as np
from jax import lax

RANK = 32
MEMBERS = 64
CELLS_DEV = 8192
OBS_DEV = 2048
CELLS = 262144
DAILY_STEPS = 24
CAP = 128
N_SPACE = 32


def draw_decay(key, part):
    random_key_list = jax.random.split(key, 4)
    slow_share = 0.5
    slow_mask = jax.random.uniform(random_key_list[0], (RANK,)) < slow_share
    jitter = jax.random.uniform(random_key_list[1], (DAILY_STEPS, RANK), minval=0.5, maxval=1.5)
    fast_scale = jax.random.uniform(random_key_list[2], (RANK,), minval=3.0, maxval=9.0)
    slow_day = jnp.exp(jitter * (math.log(0.5) / DAILY_STEPS))
    fast_day = jnp.exp(-jitter / fast_scale[None, :])
    surge_day_list = jax.random.randint(random_key_list[3], (3,), 0, DAILY_STEPS)
    surge_row_list = jnp.any(jnp.arange(DAILY_STEPS)[:, None] == surge_day_list[None, :], axis=1)
    selected_entries = jnp.where(slow_mask[None, :], slow_day, fast_day)
    return (selected_entries * jnp.where(surge_row_list, 0.6, 1.0)[:, None]).astype(jnp.float32)


def draw_background(key, part):
    key_list = jax.random.split(jax.random.fold_in(key, 17), 3)
    strength = 0.7
    own_part = jnp.clip(jax.random.normal(key_list[0], (CELLS, MEMBERS), jnp.float32), -6.0, 6.0)
    cell_factor = jnp.clip(jax.random.normal(key_list[1], (4, CELLS), jnp.float32), -4.0, 4.0)
    member_factor = jnp.clip(jax.random.normal(key_list[2], (4, MEMBERS), jnp.float32), -4.0, 4.0)
    shared_part = cell_factor[0][:, None] * member_factor[0][None, :]
    shared_part = shared_part + cell_factor[1][:, None] * member_factor[1][None, :]
    shared_part = shared_part + cell_factor[2][:, None] * member_factor[2][None, :]
    shared_part = shared_part + cell_factor[3][:, None] * member_factor[3][None, :]
    norm_factor = 1.0 / math.sqrt(MEMBERS * (1.0 + 4.0 * strength * strength))
    return ((own_part + strength * shared_part) * norm_factor).astype(jnp.bfloat16)


def touch_ends(array, key, least, largest):
    longest = array.shape.index(max(array.shape))
    spots = []
    for shift in (0, 1):
        where = [jax.random.randint(jax.random.fold_in(key, axis), (), 0, length) for axis, length in enumerate(array.shape)]
        where[longest] = (where[longest] + shift) % array.shape[longest]
        spots.append(tuple(where))
    return array.at[spots[0]].set(least).at[spots[1]].set(largest)


def steps_of(own_key, shape, pieces, smallest, top_value):
    level = 1.0
    for dim, parts in pieces:
        draws = jax.random.uniform(jax.random.fold_in(jax.random.fold_in(own_key, 6), dim), (parts,), jnp.float32, smallest / len(pieces), top_value / len(pieces))
        level = level * jnp.repeat(jnp.exp(draws), shape[dim] // parts).reshape((-1,) + (1,) * (len(shape) - 1 - dim))
    return level


def deal_out(stream_key, own, number, rows, amount, top, reach, skew):
    ranking = jax.random.permutation(stream_key, amount)
    crowded, common = shares(amount, rows * top, reach, skew, True), shares(amount, rows * top, reach, skew, False)
    places = jnp.arange(amount)

    def named(sizes, turn):
        used = int((sizes > 0).sum())
        fixed = max(1, used // 4)
        shifted = fixed + (places - fixed + turn * (used - fixed)) % max(1, amount - fixed)
        return jnp.zeros((amount,), jnp.int32).at[ranking[jnp.where(places < fixed, places, shifted)]].set(jnp.asarray(sizes, jnp.int32))

    sizes = jnp.where(number % 4 == 0, named(crowded, number // 4), named(common, number - number // 4 - 1))
    mixed = jax.random.permutation(jax.random.fold_in(own, 3), amount)
    donor, sink = mixed[0:amount // 2 * 2:2], mixed[1:amount // 2 * 2:2]
    room = jnp.minimum(sizes[donor] - 1, reach - sizes[sink]) // 2
    room = jnp.where((donor == ranking[0]) | (sink == ranking[0]) | (sizes[sink] == 0), 0, jnp.maximum(room, 0))
    shifted = jax.random.randint(jax.random.fold_in(own, 4), (amount // 2,), 0, 1 << 20) % (room + 1)
    sizes = sizes.at[donor].add(-shifted).at[sink].add(shifted)
    items = jnp.searchsorted(jnp.cumsum(sizes), jnp.arange(rows * top), side="right").astype(jnp.int32)
    grid = items.reshape(top, rows).T
    grid = grid[jax.random.permutation(jax.random.fold_in(own, 1), rows)]
    turn = jax.random.randint(jax.random.fold_in(own, 2), (rows, 1), 0, top)
    return jnp.take_along_axis(grid, (jnp.arange(top)[None, :] + turn) % top, axis=1)


def shares(amount, total, most, skew, full):
    weights = [(1 << 20) // math.isqrt(rank ** skew) + 1 for rank in range(1, amount + 1)]
    largest = most if full else min(most, max(-(-total // amount), total * weights[0] // sum(weights)))
    least = 1 if total - largest >= amount - 1 else 0
    given, spare = [largest] + [least] * (amount - 1), total - largest - least * (amount - 1)
    while spare > 0:
        movable = [i for i in range(1, amount) if given[i] < largest] or [i for i in range(1, amount) if given[i] < most]
        pool, remaining = sum([weights[i] for i in movable]), spare
        for i in movable:
            extra = min(most - given[i], max(1, remaining * weights[i] // pool), spare)
            given[i] = given[i] + extra
            spare = spare - extra
    return np.array(given)


def scatter_about(own_key, extent, deviation, reach, cuts=(), kind=jnp.bfloat16):
    values = deviation * jax.random.normal(own_key, extent, jnp.float32)
    if cuts:
        values = values * steps_of(own_key, extent, cuts, -0.22, 0.18)
    return jnp.clip(values, -reach, reach).astype(kind)


def setup_inputs(seed: int = 0) -> dict:
    splits = jax.random.split(jax.random.key(seed), 10)
    background = draw_background(jax.random.fold_in(splits[9], 71), 0)
    probe = scatter_about(splits[1], (MEMBERS, RANK), MEMBERS ** -0.5, 0.75)
    member_scale = jnp.clip(jnp.exp(jax.random.uniform(splits[2], (MEMBERS,), jnp.float32, math.log(0.5), math.log(2.0))), 0.5, 2.0)
    decay = draw_decay(jax.random.fold_in(splits[9], 71), 0)
    inflation = jnp.clip(jnp.exp(math.log(0.5) - 2.3025851 * jax.random.uniform(splits[4], (DAILY_STEPS,), jnp.float32) ** steps_of(splits[4], (DAILY_STEPS,), ((0, 8),), -0.2, 0.2)), 0.05, 0.5)
    obs_owner_keys = jax.random.split(jax.random.fold_in(splits[5], 1), DAILY_STEPS * (OBS_DEV * N_SPACE) // OBS_DEV)
    obs_owner_turns = jax.random.permutation(jax.random.fold_in(splits[5], 3), DAILY_STEPS * (OBS_DEV * N_SPACE) // OBS_DEV)
    obs_owner = jax.vmap(lambda own, number: deal_out(jax.random.fold_in(splits[5], 2), own, number, OBS_DEV, N_SPACE, 1, CAP, 2))(obs_owner_keys, obs_owner_turns).reshape((DAILY_STEPS, OBS_DEV * N_SPACE, 1))
    obs_offset = touch_ends(jax.random.randint(splits[6], (DAILY_STEPS, OBS_DEV * N_SPACE), 0, CELLS_DEV), jax.random.fold_in(splits[6], 1), 0, CELLS_DEV - 1).astype(jnp.int32)
    obs_value = scatter_about(splits[7], (DAILY_STEPS, OBS_DEV * N_SPACE), 60.0, 360.0, ((0, 8), (1, 32)), jnp.float32)
    obs_weight = jnp.clip(jnp.exp(math.log(0.002) - 2.3025852 * jax.random.uniform(splits[8], (DAILY_STEPS, OBS_DEV * N_SPACE), jnp.float32) ** steps_of(splits[8], (DAILY_STEPS, OBS_DEV * N_SPACE), ((0, 8), (1, 32)), -0.2, 0.2)), 0.0002, 0.002)
    return dict(background=background, probe=probe, member_scale=member_scale, decay=decay, inflation=inflation, obs_owner=obs_owner, obs_offset=obs_offset, obs_value=obs_value, obs_weight=obs_weight)


HIGHEST = lax.Precision.HIGHEST

def matmul_high(left_mat, right_mat):
    return jnp.matmul(left_mat, right_mat, precision=HIGHEST)

def matvec_high(matrix, vector):
    return matmul_high(matrix, vector[..., None])[..., 0]

def flip_last(matrix):
    return jnp.swapaxes(matrix, -1, -2)

def symmetric(matrix):
    return 0.5 * (matrix + flip_last(matrix))

def spd_solve(matrix, right_side):
    lower_chol = jnp.linalg.cholesky(matrix)
    middle = lax.linalg.triangular_solve(lower_chol, right_side, left_side=True, lower=True)
    return lax.linalg.triangular_solve(lower_chol, middle, left_side=True, lower=True, transpose_a=True)

def spd_inverse(matrix):
    identity_mat = jnp.broadcast_to(jnp.eye(matrix.shape[-1], dtype=jnp.float32), matrix.shape)
    return spd_solve(matrix, identity_mat)

def reference(background, probe, member_scale, decay, inflation, obs_owner, obs_offset, obs_value, obs_weight):
    scaled_probe = (probe.astype(jnp.float32) * member_scale[:, None]).astype(jnp.bfloat16)
    field_basis = jnp.dot(background.astype(jnp.float32), scaled_probe.astype(jnp.float32), preferred_element_type=jnp.float32)
    member_gram = jnp.dot(background.T.astype(jnp.float32), background.astype(jnp.float32), preferred_element_type=jnp.float32)
    probe_wide = scaled_probe.astype(jnp.float32)
    core_gram = matmul_high(matmul_high(probe_wide.T, member_gram), probe_wide)
    lower_chol = jnp.linalg.cholesky(core_gram)
    lower_inv = lax.linalg.triangular_solve(lower_chol, jnp.eye(RANK, dtype=jnp.float32), left_side=True, lower=True)
    basis = matmul_high(field_basis, lower_inv.T)
    projected = matmul_high(lower_inv, matmul_high(probe_wide.T, member_gram))
    prior_cov = matmul_high(projected * (member_scale * member_scale)[None, :], projected.T)
    cells = (obs_owner[:, :, 0] * CELLS_DEV + obs_offset).astype(jnp.int32)

    def day_info(inputs):
        cell_day, value_day, weight_day = inputs
        basis_rows = basis[cell_day]
        core_day = matmul_high((basis_rows * weight_day[:, None]).T, basis_rows)
        vector_day = matvec_high(basis_rows.T, weight_day * value_day)
        return (core_day, vector_day)
    precision_core, info_vector = lax.map(day_info, (cells, obs_value, obs_weight))

    def filter_step(carry, inputs):
        mean_prev, cov_prev = carry
        decay_day, infl_day, prec_day, vector_day = inputs
        predicted = decay_day[:, None] * cov_prev * decay_day[None, :] + infl_day * prior_cov
        pred_inv = spd_inverse(predicted)
        cov_post = symmetric(spd_inverse(pred_inv + prec_day))
        mean_post = matvec_high(cov_post, matvec_high(pred_inv, decay_day * mean_prev) + vector_day)
        return ((mean_post, cov_post), (mean_post, cov_post))
    start = (jnp.zeros((RANK,), jnp.float32), prior_cov)
    unused, (filt_mean, filtered_covariance) = lax.scan(filter_step, start, (decay, inflation, precision_core, info_vector))

    def smooth_step(carry, inputs):
        mean_next, cov_next = carry
        mean_day, cov_day, decay_next, infl_next = inputs
        predicted = decay_next[:, None] * cov_day * decay_next[None, :] + infl_next * prior_cov
        gain_day = flip_last(spd_solve(predicted, decay_next[:, None] * cov_day))
        mean_smooth = mean_day + matvec_high(gain_day, mean_next - decay_next * mean_day)
        cov_smooth = symmetric(cov_day + matmul_high(matmul_high(gain_day, cov_next - predicted), flip_last(gain_day)))
        return ((mean_smooth, cov_smooth), (mean_smooth, cov_smooth))
    last_state = (filt_mean[-1], filtered_covariance[-1])
    unused_two, (early_mean, early_cov) = lax.scan(smooth_step, last_state, (filt_mean[:-1], filtered_covariance[:-1], decay[1:], inflation[1:]), reverse=True)
    sm_mean = jnp.concatenate([early_mean, filt_mean[-1:]], axis=0)
    sm_cov = jnp.concatenate([early_cov, filtered_covariance[-1:]], axis=0)
    smooth_mean = matmul_high(sm_mean, basis.T)

    def spread_day(cov_day):
        return jnp.sum(matmul_high(basis, cov_day) * basis, axis=1)
    smooth_spread = lax.map(spread_day, sm_cov)
    return (smooth_mean, smooth_spread)
```

```python
import jax
import jax.numpy as jnp
from jax import lax
from jax.experimental import pallas as pl
from jax.experimental.pallas import tpu as pltpu
from jax.sharding import PartitionSpec as P

F32, BF16, I32 = jnp.float32, jnp.bfloat16, jnp.int32
HIGHEST = lax.Precision.HIGHEST
RANK = 32
LANES = 128
PARAMS = pltpu.CompilerParams(vmem_limit_bytes=56 << 20)


def iota(shape, dim):
    return lax.broadcasted_iota(I32, shape, dim)


def nt(a, b):
    return lax.dot_general(a, b, (((1,), (1,)), ((), ())), preferred_element_type=F32)


def nn_high(a, b):
    return lax.dot_general(
        a, b, (((1,), (0,)), ((), ())), precision=HIGHEST, preferred_element_type=F32
    )


def halves(x):
    top = x.astype(BF16).astype(F32)
    return top, x - top


def bucket_kernel(owner_ref, off_ref, val_ref, wgt_ref, bt_ref, send_ref, lhs_s, rt_s):
    days, _, obs = owner_ref.shape
    owners = send_ref.shape[0]
    chunks = obs // LANES
    upper = (iota((LANES, LANES), 0) < iota((LANES, LANES), 1)).astype(F32)
    counter = jnp.concatenate([upper, jnp.ones((LANES, LANES), F32)], axis=1).astype(BF16)
    sub_owner = iota((owners, LANES), 0)
    sub_slot = iota((LANES, LANES), 0)
    for d in range(days):
        base = jnp.zeros((owners, LANES), F32)
        for c in range(chunks):
            at = slice(c * LANES, (c + 1) * LANES)
            hit = sub_owner == owner_ref[d, :, at]
            one_hot = jnp.where(hit, 1.0, 0.0)
            counts = lax.dot_general(
                one_hot.astype(BF16), counter, (((1,), (0,)), ((), ())), preferred_element_type=F32
            )
            slot = jnp.sum(one_hot * (counts[:, :LANES] + base), axis=0, keepdims=True)
            base = base + counts[:, LANES:]
            rt_s[d, :, at] = jnp.where(sub_slot == slot.astype(I32), 1.0, 0.0).astype(BF16)
            weight = wgt_ref[d : d + 1, at]
            offset = off_ref[d : d + 1, at]
            fields = (
                *halves(weight),
                *halves(weight * val_ref[d : d + 1, at]),
                (offset >> 7).astype(F32),
                (offset & 127).astype(F32),
            )
            for f, row in enumerate(fields):
                lhs_s[d, f * owners : (f + 1) * owners, at] = jnp.where(hit, row, 0.0).astype(BF16)
    for d in range(days):
        got = nt(lhs_s[d], rt_s[d])
        part = [got[f * owners : (f + 1) * owners] for f in range(6)]
        for f, x in enumerate((part[0] + part[1], part[2] + part[3], part[4] * 128.0 + part[5])):
            j = f * days + d
            send_ref[:, j * LANES : (j + 1) * LANES] = x
    gram = nt(bt_ref[...], bt_ref[...])
    send_ref[:, 9 * LANES : 10 * LANES] = jnp.concatenate([gram[:32], gram[32:]], axis=1)


def field_kernel(bt_ref, probe_ref, scale_ref, ft_ref, fp_ref):
    scaled = (probe_ref[...].astype(F32) * scale_ref[...]).astype(BF16)
    ft = lax.dot_general(
        scaled, bt_ref[...], (((1,), (0,)), ((), ())), preferred_element_type=F32
    )
    ft_ref[...] = ft
    top = ft.astype(BF16)
    fp_ref[:32] = top
    fp_ref[32:] = (ft - top.astype(F32)).astype(BF16)


def gram_kernel(recv_ref, ft_ref, fp_ref, out_ref, w1_s, w2_s, u1_s, u2_s, off_s, lhs_s, rhs_s, wc_s, uc_s, x_s, pay_s):
    readers = recv_ref.shape[0]
    days = 3
    for d in range(days):
        w = recv_ref[:, d * LANES : (d + 1) * LANES]
        u = recv_ref[:, (3 + d) * LANES : (4 + d) * LANES]
        w1_s[d], w2_s[d] = halves(w)
        u1_s[d], u2_s[d] = halves(u)
        off_s[d] = recv_ref[:, (6 + d) * LANES : (7 + d) * LANES].astype(I32)
    sub64 = iota((64, LANES), 0)
    sub128 = iota((LANES, LANES), 0)

    def spread_reader(r, _):
        at = pl.ds(pl.multiple_of(r * LANES, LANES), LANES)
        for d in range(days):
            offset = off_s[d, pl.ds(r, 1), :]
            hit = sub64 == (offset >> 7)
            for f, ref in enumerate((w1_s, w2_s, u1_s, u2_s)):
                lhs_s[d, f * 64 : (f + 1) * 64, at] = jnp.where(
                    hit, ref[d, pl.ds(r, 1), :], 0.0
                ).astype(BF16)
            rhs_s[d, :, at] = jnp.where(sub128 == (offset & 127), 1.0, 0.0).astype(BF16)
        return 0

    lax.fori_loop(0, readers, spread_reader, 0, unroll=2)
    for d in range(days):
        got = nt(lhs_s[d], rhs_s[d])
        wc_s[d] = got[:64] + got[64:128]
        uc_s[d] = got[128:192] + got[192:]

    def weigh(h, accs):
        at = pl.ds(pl.multiple_of(h * LANES, LANES), LANES)
        ft = ft_ref[:, at]
        new = []
        for d in range(days):
            x = ft * wc_s[d, pl.ds(h, 1), :]
            top = x.astype(BF16)
            x_s[d * 64 : d * 64 + 32, at] = top
            x_s[d * 64 + 32 : d * 64 + 64, at] = (x - top.astype(F32)).astype(BF16)
            new.append(accs[d] + ft * uc_s[d, pl.ds(h, 1), :])
        return tuple(new)

    zero = jnp.zeros((RANK, LANES), F32)
    accs = lax.fori_loop(0, 64, weigh, (zero, zero, zero), unroll=2)
    prod = nt(x_s[...], fp_ref[...])
    chunk = jnp.sum(recv_ref[:, 9 * LANES : 10 * LANES], axis=0, keepdims=True)
    row16, lane16 = iota((16, LANES), 0), iota((16, LANES), 1)
    fold = jnp.where((lane16 >> 3) == row16, chunk, 0.0)
    for shift in (64, 32, 16, 8):
        fold = fold + pltpu.roll(fold, shift, 1)
    pay = jnp.where((lane16 >= 112) & (lane16 < 120), fold, 0.0)
    r16, c16 = iota((16, 16), 0), iota((16, 16), 1)
    pieces = []
    for d in range(days):
        p = prod[d * 64 : (d + 1) * 64]
        sym = p[:32, :32] + p[:32, 32:] + p[32:, :32] + p[32:, 32:]
        low = sym[16:, 16:]
        pieces += [jnp.where(r16 <= c16, sym[:16, :16], low), sym[:16, 16:]]
        diag = jnp.sum(jnp.where(r16 == c16, low, 0.0), axis=1, keepdims=True)
        g = jnp.sum(accs[d], axis=1, keepdims=True)
        pay = jnp.where(lane16 == 96 + 2 * d, g[:16], pay)
        pay = jnp.where(lane16 == 97 + 2 * d, g[16:], pay)
        pay = jnp.where(lane16 == 102 + d, diag, pay)
    pay_s[...] = pay
    for k, piece in enumerate(pieces):
        pay_s[:, 16 * k : 16 * (k + 1)] = piece
    pay = pay_s[...]
    for r in range(readers):
        out_ref[r] = pay


def total_kernel(recv_ref, decay_ref, decay_t_ref, infl_ref, out_ref):
    total = jnp.sum(recv_ref[...], axis=0)
    lane16 = iota((16, LANES), 1)
    lane1 = iota((1, LANES), 1)
    rows = []
    for d in range(3):
        total = jnp.where(lane16 == 105 + 2 * d, decay_t_ref[:16, d : d + 1], total)
        total = jnp.where(lane16 == 106 + 2 * d, decay_t_ref[16:, d : d + 1], total)
    for d in range(3):
        gamma = 1.0 / infl_ref[d]
        dec = decay_ref[d : d + 1, :]
        dec128 = jnp.concatenate([dec, dec, dec, dec], axis=1)
        rows.append(jnp.where(lane1 < 32, gamma, jnp.where(lane1 < 64, -gamma * dec128, 0.0)))
    for d in range(3):
        gamma = 1.0 / infl_ref[d]
        dec = decay_ref[d : d + 1, :]
        dec128 = jnp.concatenate([dec, dec, dec, dec], axis=1)
        rows.append(
            jnp.where(
                lane1 < 32, gamma * dec128, jnp.where((lane1 >= 64) & (lane1 < 96), -gamma, 0.0)
            )
        )
    rows.append(jnp.zeros((2, LANES), F32))
    both = jnp.concatenate([total] + rows, axis=0)
    for r in range(out_ref.shape[0]):
        out_ref[r] = both


def eliminate(mats, want_inv=False):
    sub8 = iota((8, LANES), 0)
    tiles = [[m[8 * t : 8 * t + 8] for t in range(4)] for m in mats]
    over = [[None] * 4 for _ in mats]
    invs = [[None] * 4 for _ in mats]
    for k in range(32):
        q, s = divmod(k, 8)
        for n, a in enumerate(tiles):
            row = jnp.broadcast_to(a[q][s : s + 1, :], (8, LANES))
            inv = 1.0 / jnp.broadcast_to(row[:, k : k + 1], (8, LANES))
            scaled = row * inv
            over[n][q] = scaled if s == 0 else jnp.where(sub8 >= s, scaled, over[n][q])
            if want_inv:
                invs[n][q] = inv if s == 0 else jnp.where(sub8 >= s, inv, invs[n][q])
            for t in range(q, 4):
                if t == q and s == 7:
                    continue
                col = jnp.broadcast_to(a[t][:, k : k + 1], (8, LANES))
                if t == q:
                    col = jnp.where(sub8 > s, col, 0.0)
                a[t] = a[t] - col * scaled
    u = [jnp.concatenate(a, axis=0) for a in tiles]
    v = [jnp.concatenate(a, axis=0) for a in over]
    i = [jnp.concatenate(a, axis=0) for a in invs] if want_inv else None
    return u, v, i


def tn_high(a, b):
    return nn_high(jnp.transpose(a), b)


def setup_kernel(recv_ref, probe_ref, scale_ref, ft_ref, linv_ref, bd_ref, k3_ref, b_ref):
    lane = iota((32, LANES), 1)
    gram = jnp.zeros((32, LANES), F32)
    for i in range(16):
        slab = recv_ref[:, i, :]
        moved = pltpu.roll(slab, (8 * i - 112) % LANES, 1)
        gram = jnp.where((lane >> 3) == i, moved, gram)
    gram = jnp.concatenate([gram[:, :64], gram[:, 64:]], axis=0)
    scale = scale_ref[...]
    scaled = (probe_ref[...].astype(F32) * scale).astype(BF16).astype(F32)
    half = nn_high(scaled, gram)
    core = lax.dot_general(
        half, scaled, (((1,), (1,)), ((), ())), precision=HIGHEST, preferred_element_type=F32
    )
    eye = (iota((32, 32), 0) == iota((32, 32), 1)).astype(F32)
    zero64 = jnp.zeros((32, 64), F32)
    (u,), _, (inv,) = eliminate([jnp.concatenate([core, eye, zero64], axis=1)], want_inv=True)
    linv = u[:, 32:64] * jnp.sqrt(inv[:, :32])
    projected = nn_high(linv, half)
    prior = lax.dot_general(
        projected * (scale * scale),
        projected,
        (((1,), (1,)), ((), ())),
        precision=HIGHEST,
        preferred_element_type=F32,
    )
    (u,), (v,), _ = eliminate([jnp.concatenate([prior, eye, zero64], axis=1)])
    prec = tn_high(v[:, 32:64], u[:, 32:64])
    prec = 0.5 * (prec + jnp.transpose(prec))
    linv_ref[...] = linv
    k3_ref[...] = jnp.concatenate([prec, prec, prec, jnp.zeros((32, 32), F32)], axis=1)
    lt = jnp.transpose(linv)
    zero32 = jnp.zeros((32, 32), F32)
    bd_ref[...] = jnp.concatenate(
        [
            jnp.concatenate([x if i == j else zero32 for j in range(4)], axis=1)
            for i, x in enumerate((lt, lt, lt, eye))
        ],
        axis=0,
    )
    basis = nn_high(linv, ft_ref[...])
    top = basis.astype(BF16)
    b_ref[0:32] = top
    b_ref[32:64] = (basis - top.astype(F32)).astype(BF16)
    b_ref[64:96] = top


class Eliminated:
    def __init__(self, node):
        self.node = node
        self.left = None
        self.right = None


def solve_kernel(pos_ref, recv_ref, linv_ref, bd_ref, k3_ref, b_ref, mean_ref, spread_ref, e_s, x_s):
    lane = iota((32, LANES), 1)
    k3 = k3_ref[...]
    r16, c16 = iota((16, 16), 0), iota((16, 16), 1)
    zero_row = jnp.zeros((1, LANES), F32)
    dcols = []
    for r in range(8):
        x = recv_ref[r, :16, :]
        xt = jnp.transpose(x)
        slabs = []
        for d in range(3):
            a = x[:, 32 * d : 32 * d + 16]
            q = x[:, 32 * d + 16 : 32 * d + 32]
            at = xt[32 * d : 32 * d + 16]
            qt = xt[32 * d + 16 : 32 * d + 32]
            p = jnp.where(r16 <= c16, a, at)
            low = jnp.where(r16 == c16, x[:, 102 + d : 103 + d], jnp.where(r16 > c16, a, at))
            slabs.append(
                jnp.concatenate(
                    [jnp.concatenate([p, q], axis=1), jnp.concatenate([qt, low], axis=1)], axis=0
                )
            )
            dcols.append(
                jnp.concatenate(
                    [x[:, 105 + 2 * d : 106 + 2 * d], x[:, 106 + 2 * d : 107 + 2 * d]], axis=0
                )
            )
        gs = [
            jnp.concatenate([x[:, 96 + 2 * d : 97 + 2 * d], x[:, 97 + 2 * d : 98 + 2 * d]], axis=0)
            for d in range(3)
        ]
        x_s[:, r * LANES : (r + 1) * LANES] = jnp.concatenate(
            slabs + gs + [jnp.zeros((32, 29), F32)], axis=1
        )
    z = nn_high(linv_ref[...], x_s[...])
    zs = jnp.concatenate([z[:, r * LANES : (r + 1) * LANES] for r in range(8)], axis=0)
    hs = nn_high(zs, bd_ref[...])
    first = [recv_ref[b // 3, 16 + b % 3 : 17 + b % 3, :] for b in range(24)]
    first.append(jnp.where(iota((1, LANES), 1) < 32, 1.0, 0.0))
    second = [recv_ref[b // 3, 19 + b % 3 : 20 + b % 3, :] for b in range(24)] + [zero_row]
    dcols.append(jnp.zeros((32, 1), F32))
    for b in range(25):
        nxt = (b + 1) % 25
        e = k3 * first[b] + (k3 * dcols[nxt]) * second[nxt]
        if b < 24:
            h = hs[32 * (b // 3) : 32 * (b // 3) + 32]
            d = b % 3
            mat = h if d == 0 else pltpu.roll(h, LANES - 32 * d, 1)
            vec = h if d == 0 else pltpu.roll(h, LANES - d, 1)
            e = e + jnp.where(lane < 32, mat, jnp.where(lane == 96, vec, 0.0))
        e_s[b] = e
    start = 3 * pos_ref[0]
    nodes = [e_s[lax.rem(start + j, 25)] for j in range(25)]

    plan = [
        {0: [1, 3, 5, 7, 9, 11, 13, 15, 17, 19, 21, 23], 1: [2, 6, 10, 14, 18, 22], 2: [4, 12, 20], 3: [8, 24], 4: [16]},
        {0: [3, 5, 7, 9, 11, 13, 15, 17, 19, 21, 23], 1: [2, 6, 10, 14, 18, 22, 0], 2: [4, 12, 20], 3: [8, 24], 4: [16]},
        {0: [3, 5, 7, 9, 11, 13, 15, 17, 19, 21, 23, 1], 1: [6, 10, 14, 18, 22, 0], 2: [4, 12, 20], 3: [8, 24], 4: [16]},
    ]
    rings = [[(j, j) for j in range(25)] for _ in range(3)]
    values = dict(enumerate(nodes))
    fresh = [25]
    updated = {}

    def renew(key, make):
        if key not in updated:
            values[fresh[0]] = make()
            updated[key] = fresh[0]
            fresh[0] += 1
        return updated[key]

    for level in range(5):
        todo = []
        for target in range(3):
            held = dict(rings[target])
            todo += [held[j] for j in plan[target][level] if held[j] not in todo]
        us, vs, _ = eliminate([values[i] for i in todo])
        prods = {}
        for i, u, v in zip(todo, us, vs):
            prods[i] = nn_high(jnp.transpose(v)[32:96], u)
        for target in range(3):
            ring = rings[target]
            gone = plan[target][level]
            size = len(ring)
            out = []
            for at, (j, i) in enumerate(ring):
                if j in gone:
                    continue
                pj, pi = ring[at - 1]
                nj, ni = ring[(at + 1) % size]
                key = i
                if nj in gone:
                    def as_left(i=i, ni=ni):
                        p = prods[ni][:32]
                        own = jnp.where(lane < 32, pltpu.roll(p, LANES - 32, 1), jnp.where(lane >= 64, p, 0.0))
                        kept = jnp.where((lane < 64) | (lane >= 96), values[i], 0.0)
                        return kept - own

                    i = renew(("l", i, ni), as_left)
                if pj in gone:
                    def as_right(i=i, pi=pi):
                        p = prods[pi][32:]
                        own = jnp.where(
                            lane < 32,
                            pltpu.roll(p, LANES - 64, 1),
                            jnp.where((lane < 64) | (lane >= 96), p, 0.0),
                        )
                        kept = jnp.where((lane < 32) | (lane >= 64), values[i], 0.0)
                        return kept - own

                    i = renew(("r", i, pi), as_right)
                out.append((j, i))
            rings[target] = out
    eye_at = jnp.where(lane == iota((32, LANES), 0) + 32, 1.0, 0.0)
    last = []
    for target in range(3):
        (pair,) = rings[target]
        m = values[pair[1]]
        m = m + jnp.where(lane < 32, pltpu.roll(m, LANES - 32, 1) + pltpu.roll(m, LANES - 64, 1), 0.0)
        last.append(jnp.where((lane < 32) | (lane >= 96), m, 0.0) + eye_at)
    us, vs, _ = eliminate(last)
    rows, sums = [], []
    for u, v in zip(us, vs):
        vt = jnp.transpose(v)
        cov = nn_high(vt[32:64], u)[:, 32:64]
        rows.append(cov)
        sums.append(nn_high(vt[96:104], u)[0:1, 32:64])
    lhs = jnp.concatenate(rows + sums + [jnp.zeros((5, 32), F32)], axis=0)
    one, two = halves(lhs)
    lhs = jnp.concatenate([one, one, two], axis=1).astype(BF16)
    cells = b_ref.shape[1]
    step = 512

    def finish(c, _):
        at = pl.ds(pl.multiple_of(c * step, step), step)
        b = b_ref[:, at]
        y = lax.dot_general(lhs, b, (((1,), (0,)), ((), ())), preferred_element_type=F32)
        wide = b[0:32].astype(F32) + b[32:64].astype(F32)
        for d in range(3):
            spread_ref[d : d + 1, at] = jnp.sum(y[32 * d : 32 * d + 32] * wide, axis=0, keepdims=True)
            mean_ref[d : d + 1, at] = y[96 + d : 97 + d]
        return 0

    lax.fori_loop(0, cells // step, finish, 0, unroll=2)


def shape(*dims, dtype=F32):
    return jax.ShapeDtypeStruct(dims, dtype)


def call(kernel, out, scratch=(), in_specs=None, name=None):
    extra = {} if in_specs is None else {"in_specs": in_specs}
    return pl.pallas_call(
        kernel, out_shape=out, scratch_shapes=list(scratch), compiler_params=PARAMS, name=name, **extra
    )


VM = pl.BlockSpec(memory_space=pltpu.VMEM)
SM = pl.BlockSpec(memory_space=pltpu.SMEM)


def body(
    background, probe, member_scale, decay, inflation, obs_owner, obs_offset, obs_value, obs_weight
):
    bt = background.T
    probe_t = probe.T
    scale = member_scale.reshape(1, -1)
    owner = obs_owner.transpose(0, 2, 1)
    cells = bt.shape[1]
    send = call(
        bucket_kernel,
        shape(32, 1280),
        [pltpu.VMEM((3, 192, 2048), BF16), pltpu.VMEM((3, 128, 2048), BF16)],
        name="buckets",
    )(owner, obs_offset, obs_value, obs_weight, bt)
    recv = lax.all_to_all(send, "space", 0, 0, tiled=True)
    ft, fp = call(
        field_kernel, (shape(32, cells), shape(64, cells, dtype=BF16)), name="field"
    )(bt, probe_t, scale)
    payload = call(
        gram_kernel,
        shape(32, 16, 128),
        [
            pltpu.VMEM((3, 32, 128), F32),
            pltpu.VMEM((3, 32, 128), F32),
            pltpu.VMEM((3, 32, 128), F32),
            pltpu.VMEM((3, 32, 128), F32),
            pltpu.VMEM((3, 32, 128), I32),
            pltpu.VMEM((3, 256, 4096), BF16),
            pltpu.VMEM((3, 128, 4096), BF16),
            pltpu.VMEM((3, 64, 128), F32),
            pltpu.VMEM((3, 64, 128), F32),
            pltpu.VMEM((192, cells), BF16),
            pltpu.VMEM((16, 128), F32),
        ],
        name="grams",
    )(recv, ft, fp)
    recv_2 = lax.all_to_all(payload, "space", 0, 0, tiled=True)
    both = call(total_kernel, shape(8, 24, 128), in_specs=[VM, VM, VM, SM], name="totals")(
        recv_2, decay, decay.T, inflation
    )
    recv_3 = lax.all_to_all(both, "tm", 0, 0, tiled=True)
    linv, bd, k3, basis = call(
        setup_kernel,
        (shape(32, 32), shape(128, 128), shape(32, 128), shape(96, cells, dtype=BF16)),
        name="setup",
    )(recv_2, probe_t, scale, ft)
    pos = lax.axis_index("tm").astype(I32).reshape(1)
    mean, spread = call(
        solve_kernel,
        (shape(3, cells), shape(3, cells)),
        [pltpu.VMEM((25, 32, 128), F32), pltpu.VMEM((32, 1024), F32)],
        in_specs=[SM, VM, VM, VM, VM, VM],
        name="solve",
    )(pos, recv_3, linv, bd, k3, basis)
    return mean, spread


def solution(mesh):
    return jax.shard_map(
        body,
        mesh=mesh,
        in_specs=(
            P("space", None),
            P(),
            P(),
            P("tm", None),
            P("tm"),
            P("tm", "space", None),
            P("tm", "space"),
            P("tm", "space"),
            P("tm", "space"),
        ),
        out_specs=(P("tm", "space"), P("tm", "space")),
        check_vma=False,
    )
```

```python
import jax
import jax.numpy as jnp
from jax import lax
from jax.experimental import pallas as pl
from jax.experimental.pallas import tpu as pltpu
from jax.sharding import PartitionSpec as P

F32, BF16, I32 = jnp.float32, jnp.bfloat16, jnp.int32
HIGHEST = lax.Precision.HIGHEST
RANK = 32
LANES = 128
PARAMS = pltpu.CompilerParams(vmem_limit_bytes=56 << 20)


def iota(shape, dim):
    return lax.broadcasted_iota(I32, shape, dim)


def nt(a, b):
    return lax.dot_general(a, b, (((1,), (1,)), ((), ())), preferred_element_type=F32)


def nn_high(a, b):
    return lax.dot_general(
        a, b, (((1,), (0,)), ((), ())), precision=HIGHEST, preferred_element_type=F32
    )


def halves(x):
    top = x.astype(BF16).astype(F32)
    return top, x - top


def bucket_kernel(owner_ref, off_ref, val_ref, wgt_ref, bt_ref, send_ref, lhs_s, rt_s):
    days, _, obs = owner_ref.shape
    owners = send_ref.shape[0]
    chunks = obs // LANES
    upper = (iota((LANES, LANES), 0) < iota((LANES, LANES), 1)).astype(F32)
    counter = jnp.concatenate([upper, jnp.ones((LANES, LANES), F32)], axis=1).astype(BF16)
    sub_owner = iota((owners, LANES), 0)
    sub_slot = iota((LANES, LANES), 0)
    for d in range(days):
        base = jnp.zeros((owners, LANES), F32)
        for c in range(chunks):
            at = slice(c * LANES, (c + 1) * LANES)
            hit = sub_owner == owner_ref[d, :, at]
            one_hot = jnp.where(hit, 1.0, 0.0)
            counts = lax.dot_general(
                one_hot.astype(BF16), counter, (((1,), (0,)), ((), ())), preferred_element_type=F32
            )
            slot = jnp.sum(one_hot * (counts[:, :LANES] + base), axis=0, keepdims=True)
            base = base + counts[:, LANES:]
            rt_s[d, :, at] = jnp.where(sub_slot == slot.astype(I32), 1.0, 0.0).astype(BF16)
            weight = wgt_ref[d : d + 1, at]
            offset = off_ref[d : d + 1, at]
            fields = (
                *halves(weight),
                *halves(weight * val_ref[d : d + 1, at]),
                (offset >> 7).astype(F32),
                (offset & 127).astype(F32),
            )
            for f, row in enumerate(fields):
                lhs_s[d, f * owners : (f + 1) * owners, at] = jnp.where(hit, row, 0.0).astype(BF16)
    for d in range(days):
        got = nt(lhs_s[d], rt_s[d])
        part = [got[f * owners : (f + 1) * owners] for f in range(6)]
        for f, x in enumerate((part[0] + part[1], part[2] + part[3], part[4] * 128.0 + part[5])):
            j = f * days + d
            send_ref[:, 0, j * LANES : (j + 1) * LANES] = x
    gram = nt(bt_ref[...], bt_ref[...])
    send_ref[:, 0, 9 * LANES : 10 * LANES] = jnp.concatenate([gram[:32], gram[32:]], axis=1)


def field_kernel(bt_ref, probe_ref, scale_ref, ft_ref, fp_ref):
    scaled = (probe_ref[...].astype(F32) * scale_ref[...]).astype(BF16)
    ft = lax.dot_general(
        scaled, bt_ref[...], (((1,), (0,)), ((), ())), preferred_element_type=F32
    )
    ft_ref[...] = ft
    top = ft.astype(BF16)
    fp_ref[0:32] = top
    fp_ref[32:64] = (ft - top.astype(F32)).astype(BF16)
    fp_ref[64:96] = top


def gram_kernel(recv_ref, ft_ref, fp_ref, out_ref, lhs_s, rhs_s, wc_s, uc_s, pay_s):
    readers = recv_ref.shape[0]
    days = 3
    sub64 = iota((64, LANES), 0).astype(F32).astype(BF16)
    sub128 = iota((LANES, LANES), 0).astype(F32).astype(BF16)
    zero = jnp.zeros((), BF16)

    def packed(x, r, rows):
        line = jnp.broadcast_to(x[r : r + 1], (16, LANES)).astype(BF16)
        return jnp.concatenate([line] * (rows // 16), axis=0)

    for d in range(days):
        w = halves(recv_ref[:, 0, d * LANES : (d + 1) * LANES])
        u = halves(recv_ref[:, 0, (3 + d) * LANES : (4 + d) * LANES])
        offset = recv_ref[:, 0, (6 + d) * LANES : (7 + d) * LANES].astype(I32)
        high, low = (offset >> 7).astype(F32), (offset & 127).astype(F32)
        for r in range(readers):
            at = slice(r * LANES, (r + 1) * LANES)
            hit = sub64 == packed(high, r, 64)
            for f, x in enumerate(w + u):
                lhs_s[d, f * 64 : (f + 1) * 64, at] = jnp.where(hit, packed(x, r, 64), zero)
            rhs_s[d, :, at] = jnp.where(sub128 == packed(low, r, LANES), jnp.ones((), BF16), zero)
        got = nt(lhs_s[d], rhs_s[d])
        wc_s[d] = got[:64] + got[64:128]
        uc_s[d] = got[128:192] + got[192:]
    accs = [jnp.zeros((RANK, LANES), F32)] * days
    prod = jnp.zeros((days * 64, 64), F32)
    for start in range(0, 64, 4):
        xs = []
        for h in range(start, start + 4):
            ft = ft_ref[:, h * LANES : (h + 1) * LANES]
            pieces = []
            for d in range(days):
                x = ft * wc_s[d, h : h + 1, :]
                top = x.astype(BF16)
                pieces += [top, (x - top.astype(F32)).astype(BF16)]
                accs[d] = accs[d] + ft * uc_s[d, h : h + 1, :]
            xs.append(jnp.concatenate(pieces, axis=0))
        x = jnp.concatenate(xs, axis=1)
        prod = prod + nt(x, fp_ref[0:64, start * LANES : (start + 4) * LANES])
    chunk = jnp.sum(recv_ref[:, 0, 9 * LANES : 10 * LANES], axis=0, keepdims=True)
    row16, lane16 = iota((16, LANES), 0), iota((16, LANES), 1)
    fold = jnp.where((lane16 >> 3) == row16, chunk, 0.0)
    for shift in (64, 32, 16, 8):
        fold = fold + pltpu.roll(fold, shift, 1)
    pay = jnp.where((lane16 >= 112) & (lane16 < 120), fold, 0.0)
    r16, c16 = iota((16, 16), 0), iota((16, 16), 1)
    pieces = []
    for d in range(days):
        p = prod[d * 64 : (d + 1) * 64]
        sym = p[:32, :32] + p[:32, 32:] + p[32:, :32] + p[32:, 32:]
        low = sym[16:, 16:]
        pieces += [jnp.where(r16 <= c16, sym[:16, :16], low), sym[:16, 16:]]
        diag = jnp.sum(jnp.where(r16 == c16, low, 0.0), axis=1, keepdims=True)
        g = jnp.sum(accs[d], axis=1, keepdims=True)
        pay = jnp.where(lane16 == 96 + 2 * d, g[:16], pay)
        pay = jnp.where(lane16 == 97 + 2 * d, g[16:], pay)
        pay = jnp.where(lane16 == 102 + d, diag, pay)
    pay_s[...] = pay
    for k, piece in enumerate(pieces):
        pay_s[:, 16 * k : 16 * (k + 1)] = piece
    pay = pay_s[...]
    for r in range(readers):
        out_ref[r] = pay


def total_kernel(recv_ref, decay_ref, decay_t_ref, infl_ref, out_ref):
    total = jnp.sum(recv_ref[...], axis=0)
    lane16 = iota((16, LANES), 1)
    lane1 = iota((1, LANES), 1)
    rows = []
    for d in range(3):
        total = jnp.where(lane16 == 105 + 2 * d, decay_t_ref[:16, d : d + 1], total)
        total = jnp.where(lane16 == 106 + 2 * d, decay_t_ref[16:, d : d + 1], total)
    for d in range(3):
        gamma = 1.0 / infl_ref[d]
        dec = decay_ref[d : d + 1, :]
        dec128 = jnp.concatenate([dec, dec, dec, dec], axis=1)
        rows.append(jnp.where(lane1 < 32, gamma, jnp.where(lane1 < 64, -gamma * dec128, 0.0)))
    for d in range(3):
        gamma = 1.0 / infl_ref[d]
        dec = decay_ref[d : d + 1, :]
        dec128 = jnp.concatenate([dec, dec, dec, dec], axis=1)
        rows.append(
            jnp.where(
                lane1 < 32, gamma * dec128, jnp.where((lane1 >= 64) & (lane1 < 96), -gamma, 0.0)
            )
        )
    rows.append(jnp.zeros((2, LANES), F32))
    both = jnp.concatenate([total] + rows, axis=0)
    for r in range(out_ref.shape[0]):
        out_ref[r] = both


def eliminate(mats):
    sub8 = iota((8, LANES), 0)
    low = sub8 >= 4
    tiles = [[m[8 * t : 8 * t + 8] for t in range(4)] for m in mats]
    over = [[None] * 4 for _ in mats]
    wide = lambda x: jnp.broadcast_to(x, (8, LANES))
    for k in range(0, 32, 4):
        q, s = divmod(k, 8)
        for n, a in enumerate(tiles):
            r = [wide(a[q][s + i : s + i + 1, :]) for i in range(4)]
            m = {(i, j): wide(r[i][:, k + j : k + j + 1]) for i in range(4) for j in range(i, 4)}
            ia = 1.0 / (m[0, 0] * m[1, 1] - m[0, 1] * m[0, 1])
            x02 = (m[1, 1] * m[0, 2] - m[0, 1] * m[1, 2]) * ia
            x03 = (m[1, 1] * m[0, 3] - m[0, 1] * m[1, 3]) * ia
            x12 = (m[0, 0] * m[1, 2] - m[0, 1] * m[0, 2]) * ia
            x13 = (m[0, 0] * m[1, 3] - m[0, 1] * m[0, 3]) * ia
            s22 = m[2, 2] - m[0, 2] * x02 - m[1, 2] * x12
            s23 = m[2, 3] - m[0, 2] * x03 - m[1, 2] * x13
            s33 = m[3, 3] - m[0, 3] * x03 - m[1, 3] * x13
            ib = 1.0 / (s22 * s33 - s23 * s23)
            t0 = (m[1, 1] * r[0] - m[0, 1] * r[1]) * ia
            t1 = (m[0, 0] * r[1] - m[0, 1] * r[0]) * ia
            z2 = r[2] - x02 * r[0] - x12 * r[1]
            z3 = r[3] - x03 * r[0] - x13 * r[1]
            v2 = (s33 * z2 - s23 * z3) * ib
            v3 = (s22 * z3 - s23 * z2) * ib
            v0 = t0 - x02 * v2 - x03 * v3
            v1 = t1 - x12 * v2 - x13 * v3
            v = (v0, v1, v2, v3)
            got = v0
            for i in (1, 2, 3):
                got = jnp.where(sub8 >= s + i, v[i], got)
            over[n][q] = got if s == 0 else jnp.where(low, got, over[n][q])
            for t in range(q, 4):
                if t == q and s == 4:
                    continue
                c = [wide(a[t][:, k + i : k + i + 1]) for i in range(4)]
                delta = (c[0] * v0 + c[1] * v1) + (c[2] * v2 + c[3] * v3)
                if t == q:
                    delta = jnp.where(low, delta, 0.0)
                a[t] = a[t] - delta
    u = [jnp.concatenate(a, axis=0) for a in tiles]
    v = [jnp.concatenate(a, axis=0) for a in over]
    return u, v


def finish_factor(u):
    sub8 = iota((8, LANES), 0)
    low = sub8 < 4
    within = sub8 & 3
    wide = lambda x: jnp.broadcast_to(x, (8, LANES))
    out = []
    for t in range(4):
        a = u[8 * t : 8 * t + 8]
        scale = jnp.zeros((8, LANES), F32)
        for i in range(4):
            row = jnp.where(low, wide(a[i : i + 1]), wide(a[4 + i : 5 + i]))
            at = 8 * t + i
            pivot = jnp.where(low, wide(row[:, at : at + 1]), wide(row[:, at + 4 : at + 5]))
            inv = 1.0 / pivot
            scale = jnp.where(within == i, jnp.sqrt(inv), scale)
            if i < 3:
                col = jnp.where(low, wide(a[:, at : at + 1]), wide(a[:, at + 4 : at + 5]))
                a = a - jnp.where(within > i, col * (row * inv), 0.0)
        out.append(a * scale)
    return jnp.concatenate(out, axis=0)


def tn_high(a, b):
    return nn_high(jnp.transpose(a), b)


def setup_kernel(recv_ref, probe_ref, scale_ref, fp_ref, linv_ref, bd_ref, k3_ref, b_ref):
    lane = iota((32, LANES), 1)
    gram = jnp.zeros((32, LANES), F32)
    for i in range(16):
        slab = recv_ref[:, i, :]
        moved = pltpu.roll(slab, (8 * i - 112) % LANES, 1)
        gram = jnp.where((lane >> 3) == i, moved, gram)
    gram = jnp.concatenate([gram[:, :64], gram[:, 64:]], axis=0)
    scale = scale_ref[...]
    scaled = (probe_ref[...].astype(F32) * scale).astype(BF16).astype(F32)
    half = nn_high(scaled, gram)
    core = lax.dot_general(
        half, scaled, (((1,), (1,)), ((), ())), precision=HIGHEST, preferred_element_type=F32
    )
    eye = (iota((32, 32), 0) == iota((32, 32), 1)).astype(F32)
    zero64 = jnp.zeros((32, 64), F32)
    (u,), _ = eliminate([jnp.concatenate([core, eye, zero64], axis=1)])
    linv = finish_factor(u)[:, 32:64]
    projected = nn_high(linv, half)
    prior = lax.dot_general(
        projected * (scale * scale),
        projected,
        (((1,), (1,)), ((), ())),
        precision=HIGHEST,
        preferred_element_type=F32,
    )
    (u,), (v,) = eliminate([jnp.concatenate([prior, eye, zero64], axis=1)])
    prec = tn_high(v[:, 32:64], u[:, 32:64])
    prec = 0.5 * (prec + jnp.transpose(prec))
    linv_ref[...] = linv
    k3_ref[...] = jnp.concatenate([prec, prec, prec, jnp.zeros((32, 32), F32)], axis=1)
    lt = jnp.transpose(linv)
    zero32 = jnp.zeros((32, 32), F32)
    bd_ref[...] = jnp.concatenate(
        [
            jnp.concatenate([x if i == j else zero32 for j in range(4)], axis=1)
            for i, x in enumerate((lt, lt, lt, eye))
        ],
        axis=0,
    )
    one, two = halves(linv)
    basis = lax.dot_general(
        jnp.concatenate([one, one, two], axis=1).astype(BF16),
        fp_ref[...],
        (((1,), (0,)), ((), ())),
        preferred_element_type=F32,
    )
    top = basis.astype(BF16)
    b_ref[0:32] = top
    b_ref[32:64] = (basis - top.astype(F32)).astype(BF16)
    b_ref[64:96] = top


def solve_kernel(pos_ref, recv_ref, linv_ref, bd_ref, k3_ref, b_ref, mean_ref, spread_ref, e_s, x_s):
    lane = iota((32, LANES), 1)
    k3 = k3_ref[...]
    r16, c16 = iota((16, 16), 0), iota((16, 16), 1)
    zero_row = jnp.zeros((1, LANES), F32)
    dcols = []
    for r in range(8):
        x = recv_ref[r, :16, :]
        xt = jnp.transpose(x)
        slabs = []
        for d in range(3):
            a = x[:, 32 * d : 32 * d + 16]
            q = x[:, 32 * d + 16 : 32 * d + 32]
            at = xt[32 * d : 32 * d + 16]
            qt = xt[32 * d + 16 : 32 * d + 32]
            p = jnp.where(r16 <= c16, a, at)
            low = jnp.where(r16 == c16, x[:, 102 + d : 103 + d], jnp.where(r16 > c16, a, at))
            slabs.append(
                jnp.concatenate(
                    [jnp.concatenate([p, q], axis=1), jnp.concatenate([qt, low], axis=1)], axis=0
                )
            )
            dcols.append(
                jnp.concatenate(
                    [x[:, 105 + 2 * d : 106 + 2 * d], x[:, 106 + 2 * d : 107 + 2 * d]], axis=0
                )
            )
        gs = [
            jnp.concatenate([x[:, 96 + 2 * d : 97 + 2 * d], x[:, 97 + 2 * d : 98 + 2 * d]], axis=0)
            for d in range(3)
        ]
        x_s[:, r * LANES : (r + 1) * LANES] = jnp.concatenate(
            slabs + gs + [jnp.zeros((32, 29), F32)], axis=1
        )
    z = nn_high(linv_ref[...], x_s[...])
    zs = jnp.concatenate([z[:, r * LANES : (r + 1) * LANES] for r in range(8)], axis=0)
    hs = nn_high(zs, bd_ref[...])
    first = [recv_ref[b // 3, 16 + b % 3 : 17 + b % 3, :] for b in range(24)]
    first.append(jnp.where(iota((1, LANES), 1) < 32, 1.0, 0.0))
    second = [recv_ref[b // 3, 19 + b % 3 : 20 + b % 3, :] for b in range(24)] + [zero_row]
    dcols.append(jnp.zeros((32, 1), F32))
    for b in range(25):
        nxt = (b + 1) % 25
        e = k3 * first[b] + (k3 * dcols[nxt]) * second[nxt]
        if b < 24:
            h = hs[32 * (b // 3) : 32 * (b // 3) + 32]
            d = b % 3
            mat = h if d == 0 else pltpu.roll(h, LANES - 32 * d, 1)
            vec = h if d == 0 else pltpu.roll(h, LANES - d, 1)
            e = e + jnp.where(lane < 32, mat, jnp.where(lane == 96, vec, 0.0))
        e_s[b] = e
    start = 3 * pos_ref[0]
    nodes = [e_s[lax.rem(start + j, 25)] for j in range(25)]

    plan = [
        {0: [1, 3, 5, 7, 9, 11, 13, 15, 17, 19, 21, 23], 1: [2, 6, 10, 14, 18, 22], 2: [4, 12, 20], 3: [8, 24], 4: [16]},
        {0: [3, 5, 7, 9, 11, 13, 15, 17, 19, 21, 23], 1: [2, 6, 10, 14, 18, 22, 0], 2: [4, 12, 20], 3: [8, 24], 4: [16]},
        {0: [3, 5, 7, 9, 11, 13, 15, 17, 19, 21, 23, 1], 1: [6, 10, 14, 18, 22, 0], 2: [4, 12, 20], 3: [8, 24], 4: [16]},
    ]
    rings = [[(j, j) for j in range(25)] for _ in range(3)]
    values = dict(enumerate(nodes))
    fresh = [25]
    updated = {}

    def renew(key, make):
        if key not in updated:
            values[fresh[0]] = make()
            updated[key] = fresh[0]
            fresh[0] += 1
        return updated[key]

    for level in range(5):
        todo = []
        for target in range(3):
            held = dict(rings[target])
            todo += [held[j] for j in plan[target][level] if held[j] not in todo]
        us, vs = eliminate([values[i] for i in todo])
        prods = {}
        for i, u, v in zip(todo, us, vs):
            prods[i] = nn_high(jnp.transpose(v)[32:96], u)
        for target in range(3):
            ring = rings[target]
            gone = plan[target][level]
            size = len(ring)
            out = []
            for at, (j, i) in enumerate(ring):
                if j in gone:
                    continue
                pj, pi = ring[at - 1]
                nj, ni = ring[(at + 1) % size]
                key = i
                if nj in gone:
                    def as_left(i=i, ni=ni):
                        p = prods[ni][:32]
                        own = jnp.where(lane < 32, pltpu.roll(p, LANES - 32, 1), jnp.where(lane >= 64, p, 0.0))
                        kept = jnp.where((lane < 64) | (lane >= 96), values[i], 0.0)
                        return kept - own

                    i = renew(("l", i, ni), as_left)
                if pj in gone:
                    def as_right(i=i, pi=pi):
                        p = prods[pi][32:]
                        own = jnp.where(
                            lane < 32,
                            pltpu.roll(p, LANES - 64, 1),
                            jnp.where((lane < 64) | (lane >= 96), p, 0.0),
                        )
                        kept = jnp.where((lane < 32) | (lane >= 64), values[i], 0.0)
                        return kept - own

                    i = renew(("r", i, pi), as_right)
                out.append((j, i))
            rings[target] = out
    eye_at = jnp.where(lane == iota((32, LANES), 0) + 32, 1.0, 0.0)
    last = []
    for target in range(3):
        (pair,) = rings[target]
        m = values[pair[1]]
        m = m + jnp.where(lane < 32, pltpu.roll(m, LANES - 32, 1) + pltpu.roll(m, LANES - 64, 1), 0.0)
        last.append(jnp.where((lane < 32) | (lane >= 96), m, 0.0) + eye_at)
    us, vs = eliminate(last)
    rows, sums = [], []
    for u, v in zip(us, vs):
        vt = jnp.transpose(v)
        cov = nn_high(vt[32:64], u)[:, 32:64]
        rows.append(cov)
        sums.append(nn_high(vt[96:104], u)[0:1, 32:64])
    lhs = jnp.concatenate(rows + sums + [jnp.zeros((5, 32), F32)], axis=0)
    one, two = halves(lhs)
    lhs = jnp.concatenate([one, one, two], axis=1).astype(BF16)
    cells = b_ref.shape[1]
    step = 512

    def finish(c, _):
        at = pl.ds(pl.multiple_of(c * step, step), step)
        b = b_ref[:, at]
        y = lax.dot_general(lhs, b, (((1,), (0,)), ((), ())), preferred_element_type=F32)
        wide = b[0:32].astype(F32) + b[32:64].astype(F32)
        for d in range(3):
            spread_ref[d : d + 1, at] = jnp.sum(y[32 * d : 32 * d + 32] * wide, axis=0, keepdims=True)
            mean_ref[d : d + 1, at] = y[96 + d : 97 + d]
        return 0

    lax.fori_loop(0, cells // step, finish, 0, unroll=2)


def shape(*dims, dtype=F32):
    return jax.ShapeDtypeStruct(dims, dtype)


def on_chip(*xs):
    return tuple(pltpu.with_memory_space_constraint(x, pltpu.VMEM) for x in xs)


def call(kernel, out, scratch=(), in_specs=None, name=None):
    extra = {} if in_specs is None else {"in_specs": in_specs}
    return pl.pallas_call(
        kernel, out_shape=out, scratch_shapes=list(scratch), compiler_params=PARAMS, name=name, **extra
    )


VM = pl.BlockSpec(memory_space=pltpu.VMEM)
SM = pl.BlockSpec(memory_space=pltpu.SMEM)


def body(
    background, probe, member_scale, decay, inflation, obs_owner, obs_offset, obs_value, obs_weight
):
    bt = background.T
    probe_t = probe.T
    scale = member_scale.reshape(1, -1)
    owner = obs_owner.transpose(0, 2, 1)
    cells = bt.shape[1]
    send = call(
        bucket_kernel,
        pltpu.VMEM((32, 1, 1280), F32),
        [pltpu.VMEM((3, 192, 2048), BF16), pltpu.VMEM((3, 128, 2048), BF16)],
        name="buckets",
    )(owner, obs_offset, obs_value, obs_weight, bt)
    recv = lax.all_to_all(send, "space", 0, 0, tiled=True)
    ft, fp = call(
        field_kernel, (pltpu.VMEM((32, cells), F32), pltpu.VMEM((96, cells), BF16)), name="field"
    )(bt, probe_t, scale)
    recv, ft, fp = on_chip(recv, ft, fp)
    payload = call(
        gram_kernel,
        pltpu.VMEM((32, 16, 128), F32),
        [
            pltpu.VMEM((3, 256, 4096), BF16),
            pltpu.VMEM((3, 128, 4096), BF16),
            pltpu.VMEM((3, 64, 128), F32),
            pltpu.VMEM((3, 64, 128), F32),
            pltpu.VMEM((16, 128), F32),
        ],
        name="grams",
    )(recv, ft, fp)
    recv_2 = lax.all_to_all(payload, "space", 0, 0, tiled=True)
    (recv_2,) = on_chip(recv_2)
    both = call(total_kernel, pltpu.VMEM((8, 24, 128), F32), in_specs=[VM, VM, VM, SM], name="totals")(
        recv_2, decay, decay.T, inflation
    )
    recv_3 = lax.all_to_all(both, "tm", 0, 0, tiled=True)
    (recv_3,) = on_chip(recv_3)
    linv, bd, k3, basis = call(
        setup_kernel,
        (
            pltpu.VMEM((32, 32), F32),
            pltpu.VMEM((128, 128), F32),
            pltpu.VMEM((32, 128), F32),
            pltpu.VMEM((96, cells), BF16),
        ),
        name="setup",
    )(recv_2, probe_t, scale, fp)
    linv, bd, k3, basis = on_chip(linv, bd, k3, basis)
    pos = lax.axis_index("tm").astype(I32).reshape(1)
    mean, spread = call(
        solve_kernel,
        (shape(3, cells), shape(3, cells)),
        [pltpu.VMEM((25, 32, 128), F32), pltpu.VMEM((32, 1024), F32)],
        in_specs=[SM, VM, VM, VM, VM, VM],
        name="solve",
    )(pos, recv_3, linv, bd, k3, basis)
    return mean, spread


def solution(mesh):
    return jax.shard_map(
        body,
        mesh=mesh,
        in_specs=(
            P("space", None),
            P(),
            P(),
            P("tm", None),
            P("tm"),
            P("tm", "space", None),
            P("tm", "space"),
            P("tm", "space"),
            P("tm", "space"),
        ),
        out_specs=(P("tm", "space"), P("tm", "space")),
        check_vma=False,
    )
```

```python
import jax
import jax.numpy as jnp
from jax import lax
from jax.experimental import pallas as pl
from jax.experimental.pallas import tpu as pltpu
from jax.sharding import PartitionSpec as P

F32, BF16, I32 = jnp.float32, jnp.bfloat16, jnp.int32
HIGHEST = lax.Precision.HIGHEST
RANK = 32
LANES = 128
PARAMS = pltpu.CompilerParams(vmem_limit_bytes=56 << 20)


def iota(shape, dim):
    return lax.broadcasted_iota(I32, shape, dim)


def nt(a, b):
    return lax.dot_general(a, b, (((1,), (1,)), ((), ())), preferred_element_type=F32)


def nn_high(a, b):
    return lax.dot_general(
        a, b, (((1,), (0,)), ((), ())), precision=HIGHEST, preferred_element_type=F32
    )


def halves(x):
    top = x.astype(BF16).astype(F32)
    return top, x - top


def thirds(x):
    parts = []
    for _ in range(3):
        parts.append(x.astype(BF16))
        x = x - parts[-1].astype(F32)
    return parts


def packed(line, rows):
    line = jnp.broadcast_to(line, (16, LANES)).astype(BF16)
    return jnp.concatenate([line] * (rows // 16), axis=0)


def counter16(rows):
    return iota((rows, LANES), 0).astype(F32).astype(BF16)


def bucket_kernel(owner_ref, off_ref, val_ref, wgt_ref, bt_hbm, send_ref, bt_ref, oh_s, lhs_s, rt_s, sem):
    fetch = pltpu.make_async_copy(bt_hbm, bt_ref, sem)
    fetch.start()
    days, _, obs = owner_ref.shape
    owners = send_ref.shape[0]
    chunks = obs // LANES
    upper = (iota((LANES, LANES), 0) < iota((LANES, LANES), 1)).astype(F32)
    counter = jnp.concatenate([upper, jnp.ones((LANES, LANES), F32)], axis=1).astype(BF16)
    sub_owner = counter16(owners)
    sub_slot = counter16(LANES)
    one, zero = jnp.ones((), BF16), jnp.zeros((), BF16)
    for d in range(days):
        for c in range(chunks):
            at = slice(c * LANES, (c + 1) * LANES)
            k = (d * chunks + c) * owners
            hit = sub_owner == packed(owner_ref[d, :, at].astype(F32), owners)
            oh_s[k : k + owners] = jnp.where(hit, one, zero)
    counts = jnp.dot(oh_s[...], counter, preferred_element_type=F32)
    for d in range(days):
        base = jnp.zeros((owners, LANES), F32)
        for c in range(chunks):
            at = slice(c * LANES, (c + 1) * LANES)
            k = (d * chunks + c) * owners
            one_hot = oh_s[k : k + owners]
            count = counts[k : k + owners]
            slot = jnp.sum(
                one_hot.astype(F32) * (count[:, :LANES] + base), axis=0, keepdims=True
            )
            base = base + count[:, LANES:]
            rt_s[d, :, at] = jnp.where(sub_slot == packed(slot, LANES), one, zero)
            weight = wgt_ref[d : d + 1, at]
            offset = off_ref[d : d + 1, at]
            fields = (
                *halves(weight),
                *halves(weight * val_ref[d : d + 1, at]),
                (offset >> 7).astype(F32),
                (offset & 127).astype(F32),
            )
            for f, row in enumerate(fields):
                lhs_s[d, f * owners : (f + 1) * owners, at] = one_hot * packed(row, owners)
        got = nt(lhs_s[d], rt_s[d])
        part = [got[f * owners : (f + 1) * owners] for f in range(6)]
        for f, x in enumerate((part[0] + part[1], part[2] + part[3], part[4] * 128.0 + part[5])):
            j = f * days + d
            send_ref[:, 0, j * LANES : (j + 1) * LANES] = x
    fetch.wait()
    gram = nt(bt_ref[...], bt_ref[...])
    send_ref[:, 0, 9 * LANES : 10 * LANES] = jnp.concatenate([gram[:32], gram[32:]], axis=1)


def field_kernel(bt_ref, probe_ref, scale_ref, ft_ref, fp_ref):
    scaled = (probe_ref[...].astype(F32) * scale_ref[...]).astype(BF16)
    ft = lax.dot_general(
        scaled, bt_ref[...], (((1,), (0,)), ((), ())), preferred_element_type=F32
    )
    ft_ref[...] = ft
    top = ft.astype(BF16)
    fp_ref[0:32] = top
    fp_ref[32:64] = (ft - top.astype(F32)).astype(BF16)
    fp_ref[64:96] = top


def gram_kernel(recv_ref, ft_ref, fp_ref, out_ref, lhs_s, rhs_s, wc_s, uc_s, pay_s):
    readers = recv_ref.shape[0]
    days = 3
    sub64, sub128 = counter16(64), counter16(LANES)
    one, zero = jnp.ones((), BF16), jnp.zeros((), BF16)

    for d in range(days):
        w = halves(recv_ref[:, 0, d * LANES : (d + 1) * LANES])
        u = halves(recv_ref[:, 0, (3 + d) * LANES : (4 + d) * LANES])
        offset = recv_ref[:, 0, (6 + d) * LANES : (7 + d) * LANES].astype(I32)
        high, low = (offset >> 7).astype(F32), (offset & 127).astype(F32)
        for r in range(readers):
            at = slice(r * LANES, (r + 1) * LANES)
            hit = sub64 == packed(high[r : r + 1], 64)
            for f, x in enumerate(w + u):
                lhs_s[d, f * 64 : (f + 1) * 64, at] = jnp.where(hit, packed(x[r : r + 1], 64), zero)
            rhs_s[d, :, at] = jnp.where(sub128 == packed(low[r : r + 1], LANES), one, zero)
        got = nt(lhs_s[d], rhs_s[d])
        wc_s[d] = got[:64] + got[64:128]
        uc_s[d] = got[128:192] + got[192:]
    accs = [jnp.zeros((RANK, LANES), F32)] * days
    prod = jnp.zeros((days * 64, 64), F32)
    for start in range(0, 64, 4):
        xs = []
        for h in range(start, start + 4):
            ft = ft_ref[:, h * LANES : (h + 1) * LANES]
            pieces = []
            for d in range(days):
                x = ft * wc_s[d, h : h + 1, :]
                top = x.astype(BF16)
                pieces += [top, (x - top.astype(F32)).astype(BF16)]
                accs[d] = accs[d] + ft * uc_s[d, h : h + 1, :]
            xs.append(jnp.concatenate(pieces, axis=0))
        x = jnp.concatenate(xs, axis=1)
        prod = prod + nt(x, fp_ref[0:64, start * LANES : (start + 4) * LANES])
    chunk = jnp.sum(recv_ref[:, 0, 9 * LANES : 10 * LANES], axis=0, keepdims=True)
    row16, lane16 = iota((16, LANES), 0), iota((16, LANES), 1)
    fold = jnp.where((lane16 >> 3) == row16, chunk, 0.0)
    for shift in (64, 32, 16, 8):
        fold = fold + pltpu.roll(fold, shift, 1)
    pay = jnp.where((lane16 >= 112) & (lane16 < 120), fold, 0.0)
    r16, c16 = iota((16, 16), 0), iota((16, 16), 1)
    pieces = []
    for d in range(days):
        p = prod[d * 64 : (d + 1) * 64]
        sym = p[:32, :32] + p[:32, 32:] + p[32:, :32] + p[32:, 32:]
        low = sym[16:, 16:]
        pieces += [jnp.where(r16 <= c16, sym[:16, :16], low), sym[:16, 16:]]
        diag = jnp.sum(jnp.where(r16 == c16, low, 0.0), axis=1, keepdims=True)
        g = jnp.sum(accs[d], axis=1, keepdims=True)
        pay = jnp.where(lane16 == 96 + 2 * d, g[:16], pay)
        pay = jnp.where(lane16 == 97 + 2 * d, g[16:], pay)
        pay = jnp.where(lane16 == 102 + d, diag, pay)
    pay_s[...] = pay
    for k, piece in enumerate(pieces):
        pay_s[:, 16 * k : 16 * (k + 1)] = piece
    pay = pay_s[...]
    for r in range(readers):
        out_ref[r] = pay


def total_kernel(recv_ref, decay_ref, decay_t_ref, infl_ref, out_ref):
    total = jnp.sum(recv_ref[...], axis=0)
    lane16 = iota((16, LANES), 1)
    lane1 = iota((1, LANES), 1)
    rows = []
    for d in range(3):
        total = jnp.where(lane16 == 105 + 2 * d, decay_t_ref[:16, d : d + 1], total)
        total = jnp.where(lane16 == 106 + 2 * d, decay_t_ref[16:, d : d + 1], total)
    for d in range(3):
        gamma = 1.0 / infl_ref[d]
        dec = decay_ref[d : d + 1, :]
        dec128 = jnp.concatenate([dec, dec, dec, dec], axis=1)
        rows.append(jnp.where(lane1 < 32, gamma, jnp.where(lane1 < 64, -gamma * dec128, 0.0)))
    for d in range(3):
        gamma = 1.0 / infl_ref[d]
        dec = decay_ref[d : d + 1, :]
        dec128 = jnp.concatenate([dec, dec, dec, dec], axis=1)
        rows.append(
            jnp.where(
                lane1 < 32, gamma * dec128, jnp.where((lane1 >= 64) & (lane1 < 96), -gamma, 0.0)
            )
        )
    rows.append(jnp.zeros((2, LANES), F32))
    both = jnp.concatenate([total] + rows, axis=0)
    for r in range(out_ref.shape[0]):
        out_ref[r] = both


def eliminate(mats):
    sub8 = iota((8, LANES), 0)
    low = sub8 >= 4
    tiles = [[m[8 * t : 8 * t + 8] for t in range(4)] for m in mats]
    over = [[None] * 4 for _ in mats]
    wide = lambda x: jnp.broadcast_to(x, (8, LANES))
    for k in range(0, 32, 4):
        q, s = divmod(k, 8)
        for n, a in enumerate(tiles):
            r = [wide(a[q][s + i : s + i + 1, :]) for i in range(4)]
            cq = [jnp.maximum(wide(a[q][:, k + i : k + i + 1]), -jnp.inf) for i in range(4)]
            m = {(i, j): wide(cq[j][s + i : s + i + 1, :]) for i in range(4) for j in range(i, 4)}
            ia = 1.0 / (m[0, 0] * m[1, 1] - m[0, 1] * m[0, 1])
            x02 = (m[1, 1] * m[0, 2] - m[0, 1] * m[1, 2]) * ia
            x03 = (m[1, 1] * m[0, 3] - m[0, 1] * m[1, 3]) * ia
            x12 = (m[0, 0] * m[1, 2] - m[0, 1] * m[0, 2]) * ia
            x13 = (m[0, 0] * m[1, 3] - m[0, 1] * m[0, 3]) * ia
            s22 = m[2, 2] - m[0, 2] * x02 - m[1, 2] * x12
            s23 = m[2, 3] - m[0, 2] * x03 - m[1, 2] * x13
            s33 = m[3, 3] - m[0, 3] * x03 - m[1, 3] * x13
            ib = 1.0 / (s22 * s33 - s23 * s23)
            t0 = (m[1, 1] * r[0] - m[0, 1] * r[1]) * ia
            t1 = (m[0, 0] * r[1] - m[0, 1] * r[0]) * ia
            z2 = r[2] - x02 * r[0] - x12 * r[1]
            z3 = r[3] - x03 * r[0] - x13 * r[1]
            v2 = (s33 * z2 - s23 * z3) * ib
            v3 = (s22 * z3 - s23 * z2) * ib
            v0 = t0 - x02 * v2 - x03 * v3
            v1 = t1 - x12 * v2 - x13 * v3
            v = (v0, v1, v2, v3)
            got = v0
            for i in (1, 2, 3):
                got = jnp.where(sub8 >= s + i, v[i], got)
            over[n][q] = got if s == 0 else jnp.where(low, got, over[n][q])
            for t in range(q, 4):
                if t == q and s == 4:
                    continue
                c = cq if t == q else [wide(a[t][:, k + i : k + i + 1]) for i in range(4)]
                delta = (c[0] * v0 + c[1] * v1) + (c[2] * v2 + c[3] * v3)
                if t == q:
                    delta = jnp.where(low, delta, 0.0)
                a[t] = a[t] - delta
    u = [jnp.concatenate(a, axis=0) for a in tiles]
    v = [jnp.concatenate(a, axis=0) for a in over]
    return u, v


def finish_factor(u):
    sub8 = iota((8, LANES), 0)
    low = sub8 < 4
    within = sub8 & 3
    wide = lambda x: jnp.broadcast_to(x, (8, LANES))
    out = []
    for t in range(4):
        a = u[8 * t : 8 * t + 8]
        scale = jnp.zeros((8, LANES), F32)
        for i in range(4):
            row = jnp.where(low, wide(a[i : i + 1]), wide(a[4 + i : 5 + i]))
            at = 8 * t + i
            pivot = jnp.where(low, wide(row[:, at : at + 1]), wide(row[:, at + 4 : at + 5]))
            inv = 1.0 / pivot
            scale = jnp.where(within == i, jnp.sqrt(inv), scale)
            if i < 3:
                col = jnp.where(low, wide(a[:, at : at + 1]), wide(a[:, at + 4 : at + 5]))
                a = a - jnp.where(within > i, col * (row * inv), 0.0)
        out.append(a * scale)
    return jnp.concatenate(out, axis=0)


def tn_high(a, b):
    return nn_high(jnp.transpose(a), b)


def setup_kernel(recv_ref, probe_ref, scale_ref, fp_ref, b_ref):
    lane = iota((32, LANES), 1)
    gram = jnp.zeros((32, LANES), F32)
    for i in range(16):
        slab = recv_ref[:, i, :]
        moved = pltpu.roll(slab, (8 * i - 112) % LANES, 1)
        gram = jnp.where((lane >> 3) == i, moved, gram)
    gram = jnp.concatenate([gram[:, :64], gram[:, 64:]], axis=0)
    scale = scale_ref[...]
    scaled = (probe_ref[...].astype(F32) * scale).astype(BF16).astype(F32)
    half = nn_high(scaled, gram)
    core = lax.dot_general(
        half, scaled, (((1,), (1,)), ((), ())), precision=HIGHEST, preferred_element_type=F32
    )
    eye = (iota((32, 32), 0) == iota((32, 32), 1)).astype(F32)
    zero64 = jnp.zeros((32, 64), F32)
    (u,), _ = eliminate([jnp.concatenate([core, eye, zero64], axis=1)])
    linv = finish_factor(u)[:, 32:64]
    projected = nn_high(linv, half)
    prior = lax.dot_general(
        projected * (scale * scale),
        projected,
        (((1,), (1,)), ((), ())),
        precision=HIGHEST,
        preferred_element_type=F32,
    )
    (u,), (v,) = eliminate([jnp.concatenate([prior, eye, zero64], axis=1)])
    prec = tn_high(v[:, 32:64], u[:, 32:64])
    prec = 0.5 * (prec + jnp.transpose(prec))
    cells = fp_ref.shape[1]
    zero64 = jnp.zeros((32, 64), F32)
    for k, part in enumerate(thirds(jnp.concatenate([linv, prec, zero64], axis=1))):
        b_ref[32 * k : 32 * k + 32, cells:] = part
    one, two = halves(linv)
    basis = lax.dot_general(
        jnp.concatenate([one, one, two], axis=1).astype(BF16),
        fp_ref[...],
        (((1,), (0,)), ((), ())),
        preferred_element_type=F32,
    )
    top = basis.astype(BF16)
    b_ref[0:32, :cells] = top
    b_ref[32:64, :cells] = (basis - top.astype(F32)).astype(BF16)
    b_ref[64:96, :cells] = top


def solve_kernel(pos_ref, recv_ref, b_ref, mean_ref, spread_ref, e_s, x_s):
    lane = iota((32, LANES), 1)
    cells = b_ref.shape[1] - LANES
    small = b_ref[0:32, cells:].astype(F32) + b_ref[32:64, cells:].astype(F32)
    small = small + b_ref[64:96, cells:].astype(F32)
    linv, prec = small[:, :32], small[:, 32:64]
    lt = jnp.transpose(linv)
    zero32 = jnp.zeros((32, 32), F32)
    eye = (iota((32, 32), 0) == iota((32, 32), 1)).astype(F32)
    k3 = jnp.concatenate([prec, prec, prec, zero32], axis=1)
    per_day = jnp.concatenate(
        [
            jnp.concatenate([x if i == j else zero32 for j in range(4)], axis=1)
            for i, x in enumerate((lt, lt, lt, eye))
        ],
        axis=0,
    )
    r16, c16 = iota((16, 16), 0), iota((16, 16), 1)
    zero_row = jnp.zeros((1, LANES), F32)
    dcols = []
    for r in range(8):
        x = recv_ref[r, :16, :]
        xt = jnp.transpose(x)
        slabs = []
        for d in range(3):
            a = x[:, 32 * d : 32 * d + 16]
            q = x[:, 32 * d + 16 : 32 * d + 32]
            at = xt[32 * d : 32 * d + 16]
            qt = xt[32 * d + 16 : 32 * d + 32]
            p = jnp.where(r16 <= c16, a, at)
            low = jnp.where(r16 == c16, x[:, 102 + d : 103 + d], jnp.where(r16 > c16, a, at))
            slabs.append(
                jnp.concatenate(
                    [jnp.concatenate([p, q], axis=1), jnp.concatenate([qt, low], axis=1)], axis=0
                )
            )
            dcols.append(
                jnp.concatenate(
                    [x[:, 105 + 2 * d : 106 + 2 * d], x[:, 106 + 2 * d : 107 + 2 * d]], axis=0
                )
            )
        gs = [
            jnp.concatenate([x[:, 96 + 2 * d : 97 + 2 * d], x[:, 97 + 2 * d : 98 + 2 * d]], axis=0)
            for d in range(3)
        ]
        x_s[:, r * LANES : (r + 1) * LANES] = jnp.concatenate(
            slabs + gs + [jnp.zeros((32, 29), F32)], axis=1
        )
    z = nn_high(linv, x_s[...])
    zs = jnp.concatenate([z[:, r * LANES : (r + 1) * LANES] for r in range(8)], axis=0)
    hs = nn_high(zs, per_day)
    first = [recv_ref[b // 3, 16 + b % 3 : 17 + b % 3, :] for b in range(24)]
    first.append(jnp.where(iota((1, LANES), 1) < 32, 1.0, 0.0))
    second = [recv_ref[b // 3, 19 + b % 3 : 20 + b % 3, :] for b in range(24)] + [zero_row]
    dcols.append(jnp.zeros((32, 1), F32))
    for b in range(25):
        nxt = (b + 1) % 25
        e = k3 * first[b] + (k3 * dcols[nxt]) * second[nxt]
        if b < 24:
            h = hs[32 * (b // 3) : 32 * (b // 3) + 32]
            d = b % 3
            mat = h if d == 0 else pltpu.roll(h, LANES - 32 * d, 1)
            vec = h if d == 0 else pltpu.roll(h, LANES - d, 1)
            e = e + jnp.where(lane < 32, mat, jnp.where(lane == 96, vec, 0.0))
        e_s[b] = e
    start = 3 * pos_ref[0]
    nodes = [e_s[lax.rem(start + j, 25)] for j in range(25)]

    plan = [
        {0: [1, 3, 5, 7, 9, 11, 13, 15, 17, 19, 21, 23], 1: [2, 6, 10, 14, 18, 22], 2: [4, 12, 20], 3: [8, 24], 4: [16]},
        {0: [3, 5, 7, 9, 11, 13, 15, 17, 19, 21, 23], 1: [2, 6, 10, 14, 18, 22, 0], 2: [4, 12, 20], 3: [8, 24], 4: [16]},
        {0: [3, 5, 7, 9, 11, 13, 15, 17, 19, 21, 23, 1], 1: [6, 10, 14, 18, 22, 0], 2: [4, 12, 20], 3: [8, 24], 4: [16]},
    ]
    rings = [[(j, j) for j in range(25)] for _ in range(3)]
    values = dict(enumerate(nodes))
    fresh = [25]
    updated = {}

    def renew(key, make):
        if key not in updated:
            values[fresh[0]] = make()
            updated[key] = fresh[0]
            fresh[0] += 1
        return updated[key]

    for level in range(5):
        todo = []
        for target in range(3):
            held = dict(rings[target])
            todo += [held[j] for j in plan[target][level] if held[j] not in todo]
        us, vs = eliminate([values[i] for i in todo])
        prods = {}
        for i, u, v in zip(todo, us, vs):
            prods[i] = nn_high(jnp.transpose(v)[32:96], u)
        for target in range(3):
            ring = rings[target]
            gone = plan[target][level]
            size = len(ring)
            out = []
            for at, (j, i) in enumerate(ring):
                if j in gone:
                    continue
                pj, pi = ring[at - 1]
                nj, ni = ring[(at + 1) % size]
                key = i
                if nj in gone:
                    def as_left(i=i, ni=ni):
                        p = prods[ni][:32]
                        own = jnp.where(lane < 32, pltpu.roll(p, LANES - 32, 1), jnp.where(lane >= 64, p, 0.0))
                        kept = jnp.where((lane < 64) | (lane >= 96), values[i], 0.0)
                        return kept - own

                    i = renew(("l", i, ni), as_left)
                if pj in gone:
                    def as_right(i=i, pi=pi):
                        p = prods[pi][32:]
                        own = jnp.where(
                            lane < 32,
                            pltpu.roll(p, LANES - 64, 1),
                            jnp.where((lane < 64) | (lane >= 96), p, 0.0),
                        )
                        kept = jnp.where((lane < 32) | (lane >= 64), values[i], 0.0)
                        return kept - own

                    i = renew(("r", i, pi), as_right)
                out.append((j, i))
            rings[target] = out
    eye_at = jnp.where(lane == iota((32, LANES), 0) + 32, 1.0, 0.0)
    last = []
    for target in range(3):
        (pair,) = rings[target]
        m = values[pair[1]]
        m = m + jnp.where(lane < 32, pltpu.roll(m, LANES - 32, 1) + pltpu.roll(m, LANES - 64, 1), 0.0)
        last.append(jnp.where((lane < 32) | (lane >= 96), m, 0.0) + eye_at)
    us, vs = eliminate(last)
    rows, sums = [], []
    for u, v in zip(us, vs):
        vt = jnp.transpose(v)
        cov = nn_high(vt[32:64], u)[:, 32:64]
        rows.append(cov)
        sums.append(nn_high(vt[96:104], u)[0:1, 32:64])
    lhs = jnp.concatenate(rows + sums + [jnp.zeros((5, 32), F32)], axis=0)
    one, two = halves(lhs)
    lhs = jnp.concatenate([one, one, two], axis=1).astype(BF16)
    step = 1024
    for c in range(0, cells, step):
        b = b_ref[:, c : c + step]
        y = lax.dot_general(lhs, b, (((1,), (0,)), ((), ())), preferred_element_type=F32)
        wide = b[0:32].astype(F32) + b[32:64].astype(F32)
        for d in range(3):
            spread_ref[d : d + 1, c : c + step] = jnp.sum(
                y[32 * d : 32 * d + 32] * wide, axis=0, keepdims=True
            )
        mean_ref[:, c : c + step] = y[96:99]


def shape(*dims, dtype=F32):
    return jax.ShapeDtypeStruct(dims, dtype)


def on_chip(*xs):
    return tuple(pltpu.with_memory_space_constraint(x, pltpu.VMEM) for x in xs)


def call(kernel, out, scratch=(), in_specs=None, name=None):
    extra = {} if in_specs is None else {"in_specs": in_specs}
    return pl.pallas_call(
        kernel, out_shape=out, scratch_shapes=list(scratch), compiler_params=PARAMS, name=name, **extra
    )


VM = pl.BlockSpec(memory_space=pltpu.VMEM)
SM = pl.BlockSpec(memory_space=pltpu.SMEM)


def body(
    background, probe, member_scale, decay, inflation, obs_owner, obs_offset, obs_value, obs_weight
):
    bt = background.T
    probe_t = probe.T
    scale = member_scale.reshape(1, -1)
    owner = obs_owner.transpose(0, 2, 1)
    cells = bt.shape[1]
    send = call(
        bucket_kernel,
        pltpu.VMEM((32, 1, 1280), F32),
        [
            pltpu.VMEM(bt.shape, BF16),
            pltpu.VMEM((3 * 16 * 32, 128), BF16),
            pltpu.VMEM((3, 192, 2048), BF16),
            pltpu.VMEM((3, 128, 2048), BF16),
            pltpu.SemaphoreType.DMA,
        ],
        in_specs=[VM, VM, VM, VM, pl.BlockSpec(memory_space=pl.ANY)],
        name="buckets",
    )(owner, obs_offset, obs_value, obs_weight, bt)
    recv = lax.all_to_all(send, "space", 0, 0, tiled=True)
    ft, fp = call(
        field_kernel, (pltpu.VMEM((32, cells), F32), pltpu.VMEM((96, cells), BF16)), name="field"
    )(bt, probe_t, scale)
    recv, ft, fp = on_chip(recv, ft, fp)
    payload = call(
        gram_kernel,
        pltpu.VMEM((32, 16, 128), F32),
        [
            pltpu.VMEM((3, 256, 4096), BF16),
            pltpu.VMEM((3, 128, 4096), BF16),
            pltpu.VMEM((3, 64, 128), F32),
            pltpu.VMEM((3, 64, 128), F32),
            pltpu.VMEM((16, 128), F32),
        ],
        name="grams",
    )(recv, ft, fp)
    recv_2 = lax.all_to_all(payload, "space", 0, 0, tiled=True)
    (recv_2,) = on_chip(recv_2)
    both = call(total_kernel, pltpu.VMEM((8, 24, 128), F32), in_specs=[VM, VM, VM, SM], name="totals")(
        recv_2, decay, decay.T, inflation
    )
    recv_3 = lax.all_to_all(both, "tm", 0, 0, tiled=True)
    (recv_3,) = on_chip(recv_3)
    basis = call(
        setup_kernel,
        pltpu.VMEM((96, cells + 128), BF16),
        name="setup",
    )(recv_2, probe_t, scale, fp)
    (basis,) = on_chip(basis)
    pos = lax.axis_index("tm").astype(I32).reshape(1)
    mean, spread = call(
        solve_kernel,
        (shape(3, cells), shape(3, cells)),
        [pltpu.VMEM((25, 32, 128), F32), pltpu.VMEM((32, 1024), F32)],
        in_specs=[SM, VM, VM],
        name="solve",
    )(pos, recv_3, basis)
    return mean, spread


def solution(mesh):
    return jax.shard_map(
        body,
        mesh=mesh,
        in_specs=(
            P("space", None),
            P(),
            P(),
            P("tm", None),
            P("tm"),
            P("tm", "space", None),
            P("tm", "space"),
            P("tm", "space"),
            P("tm", "space"),
        ),
        out_specs=(P("tm", "space"), P("tm", "space")),
        check_vma=False,
    )
```

```python
import jax
import jax.numpy as jnp
from jax import lax
from jax.experimental import pallas as pl
from jax.experimental.pallas import tpu as pltpu
from jax.sharding import PartitionSpec as P

F32, BF16, I32 = jnp.float32, jnp.bfloat16, jnp.int32
HIGHEST = lax.Precision.HIGHEST
RANK = 32
LANES = 128
PARAMS = pltpu.CompilerParams(vmem_limit_bytes=56 << 20)


def iota(shape, dim):
    return lax.broadcasted_iota(I32, shape, dim)


def nt(a, b):
    return lax.dot_general(a, b, (((1,), (1,)), ((), ())), preferred_element_type=F32)


def nn_high(a, b):
    return lax.dot_general(
        a, b, (((1,), (0,)), ((), ())), precision=HIGHEST, preferred_element_type=F32
    )


def halves(x):
    top = x.astype(BF16).astype(F32)
    return top, x - top


def thirds(x):
    parts = []
    for _ in range(3):
        parts.append(x.astype(BF16))
        x = x - parts[-1].astype(F32)
    return parts


def packed(line, rows):
    line = jnp.broadcast_to(line, (16, LANES)).astype(BF16)
    return jnp.concatenate([line] * (rows // 16), axis=0)


def counter16(rows):
    return iota((rows, LANES), 0).astype(F32).astype(BF16)


def bucket_kernel(owner_ref, off_ref, val_ref, wgt_ref, bt_hbm, send_ref, bt_ref, oh_s, lhs_s, rt_s, sem):
    fetch = pltpu.make_async_copy(bt_hbm, bt_ref, sem)
    fetch.start()
    days, _, obs = owner_ref.shape
    owners = send_ref.shape[0]
    chunks = obs // LANES
    upper = (iota((LANES, LANES), 0) < iota((LANES, LANES), 1)).astype(F32)
    counter = jnp.concatenate([upper, jnp.ones((LANES, LANES), F32)], axis=1).astype(BF16)
    sub_owner = counter16(owners)
    sub_slot = counter16(LANES)
    one, zero = jnp.ones((), BF16), jnp.zeros((), BF16)
    for d in range(days):
        for c in range(chunks):
            at = slice(c * LANES, (c + 1) * LANES)
            k = (d * chunks + c) * owners
            hit = sub_owner == packed(owner_ref[d, :, at].astype(F32), owners)
            oh_s[k : k + owners] = jnp.where(hit, one, zero)
    counts = jnp.dot(oh_s[...], counter, preferred_element_type=F32)
    for d in range(days):
        base = jnp.zeros((owners, LANES), F32)
        for c in range(chunks):
            at = slice(c * LANES, (c + 1) * LANES)
            k = (d * chunks + c) * owners
            one_hot = oh_s[k : k + owners]
            count = counts[k : k + owners]
            slot = jnp.sum(
                one_hot.astype(F32) * (count[:, :LANES] + base), axis=0, keepdims=True
            )
            base = base + count[:, LANES:]
            rt_s[d, :, at] = jnp.where(sub_slot == packed(slot, LANES), one, zero)
            weight = wgt_ref[d : d + 1, at]
            offset = off_ref[d : d + 1, at]
            fields = (
                *halves(weight),
                *halves(weight * val_ref[d : d + 1, at]),
                (offset >> 7).astype(F32),
                (offset & 127).astype(F32),
            )
            for f, row in enumerate(fields):
                lhs_s[d, f * owners : (f + 1) * owners, at] = one_hot * packed(row, owners)
        got = nt(lhs_s[d], rt_s[d])
        part = [got[f * owners : (f + 1) * owners] for f in range(6)]
        for f, x in enumerate((part[0] + part[1], part[2] + part[3], part[4] * 128.0 + part[5])):
            j = f * days + d
            send_ref[:, 0, j * LANES : (j + 1) * LANES] = x
    fetch.wait()
    gram = nt(bt_ref[...], bt_ref[...])
    send_ref[:, 0, 9 * LANES : 10 * LANES] = jnp.concatenate([gram[:32], gram[32:]], axis=1)


def field_kernel(
    bt_ref, probe_ref, scale_ref, decay_ref, decay_t_ref, infl_ref, ft_ref, fp_ref, probe_out, days_ref
):
    scale = scale_ref[...]
    scaled = (probe_ref[...].astype(F32) * scale).astype(BF16)
    ft = jnp.dot(scaled, bt_ref[...], preferred_element_type=F32)
    ft_ref[...] = ft
    top = ft.astype(BF16)
    fp_ref[0:32] = top
    fp_ref[32:64] = (ft - top.astype(F32)).astype(BF16)
    fp_ref[64:96] = top
    probe_out[0:32] = scaled.astype(F32)
    probe_out[32:40] = jnp.broadcast_to(scale * scale, (8, scale.shape[1]))
    lane16, lane1 = iota((16, LANES), 1), iota((1, LANES), 1)
    columns = jnp.zeros((16, LANES), F32)
    first, second = [], []
    for d in range(3):
        columns = jnp.where(lane16 == 105 + 2 * d, decay_t_ref[:16, d : d + 1], columns)
        columns = jnp.where(lane16 == 106 + 2 * d, decay_t_ref[16:, d : d + 1], columns)
        gamma = 1.0 / infl_ref[d]
        decay = jnp.concatenate([decay_ref[d : d + 1, :]] * 4, axis=1)
        right = (lane1 >= 64) & (lane1 < 96)
        first.append(jnp.where(lane1 < 32, gamma, jnp.where(lane1 < 64, -gamma * decay, 0.0)))
        second.append(jnp.where(lane1 < 32, gamma * decay, jnp.where(right, -gamma, 0.0)))
    rows = first + second + [jnp.zeros((2, LANES), F32)]
    days_ref[...] = jnp.concatenate([columns] + rows, axis=0)


def gram_kernel(recv_ref, ft_ref, fp_ref, out_ref, lhs_s, rhs_s, wc_s, uc_s, pay_s):
    readers = recv_ref.shape[0]
    days = 3
    sub64, sub128 = counter16(64), counter16(LANES)
    one, zero = jnp.ones((), BF16), jnp.zeros((), BF16)

    for d in range(days):
        w = halves(recv_ref[:, 0, d * LANES : (d + 1) * LANES])
        u = halves(recv_ref[:, 0, (3 + d) * LANES : (4 + d) * LANES])
        offset = recv_ref[:, 0, (6 + d) * LANES : (7 + d) * LANES].astype(I32)
        high, low = (offset >> 7).astype(F32), (offset & 127).astype(F32)
        for r in range(readers):
            at = slice(r * LANES, (r + 1) * LANES)
            hit = sub64 == packed(high[r : r + 1], 64)
            for f, x in enumerate(w + u):
                lhs_s[d, f * 64 : (f + 1) * 64, at] = jnp.where(hit, packed(x[r : r + 1], 64), zero)
            rhs_s[d, :, at] = jnp.where(sub128 == packed(low[r : r + 1], LANES), one, zero)
        got = nt(lhs_s[d], rhs_s[d])
        wc_s[d] = got[:64] + got[64:128]
        uc_s[d] = got[128:192] + got[192:]
    accs = [jnp.zeros((RANK, LANES), F32)] * days
    prod = jnp.zeros((days * 64, 64), F32)
    for start in range(0, 64, 4):
        xs = []
        for h in range(start, start + 4):
            ft = ft_ref[:, h * LANES : (h + 1) * LANES]
            pieces = []
            for d in range(days):
                x = ft * wc_s[d, h : h + 1, :]
                top = x.astype(BF16)
                pieces += [top, (x - top.astype(F32)).astype(BF16)]
                accs[d] = accs[d] + ft * uc_s[d, h : h + 1, :]
            xs.append(jnp.concatenate(pieces, axis=0))
        x = jnp.concatenate(xs, axis=1)
        prod = prod + nt(x, fp_ref[0:64, start * LANES : (start + 4) * LANES])
    chunk = jnp.sum(recv_ref[:, 0, 9 * LANES : 10 * LANES], axis=0, keepdims=True)
    row16, lane16 = iota((16, LANES), 0), iota((16, LANES), 1)
    fold = jnp.where((lane16 >> 3) == row16, chunk, 0.0)
    for shift in (64, 32, 16, 8):
        fold = fold + pltpu.roll(fold, shift, 1)
    pay = jnp.where((lane16 >= 112) & (lane16 < 120), fold, 0.0)
    r16, c16 = iota((16, 16), 0), iota((16, 16), 1)
    pieces = []
    for d in range(days):
        p = prod[d * 64 : (d + 1) * 64]
        sym = p[:32, :32] + p[:32, 32:] + p[32:, :32] + p[32:, 32:]
        low = sym[16:, 16:]
        pieces += [jnp.where(r16 <= c16, sym[:16, :16], low), sym[:16, 16:]]
        diag = jnp.sum(jnp.where(r16 == c16, low, 0.0), axis=1, keepdims=True)
        g = jnp.sum(accs[d], axis=1, keepdims=True)
        pay = jnp.where(lane16 == 96 + 2 * d, g[:16], pay)
        pay = jnp.where(lane16 == 97 + 2 * d, g[16:], pay)
        pay = jnp.where(lane16 == 102 + d, diag, pay)
    pay_s[...] = pay
    for k, piece in enumerate(pieces):
        pay_s[:, 16 * k : 16 * (k + 1)] = piece
    pay = pay_s[...]
    for r in range(readers):
        out_ref[r] = pay


def total_kernel(recv_ref, days_ref, out_ref):
    total = jnp.sum(recv_ref[...], axis=0)
    both = days_ref[...] + jnp.concatenate([total, jnp.zeros((8, LANES), F32)], axis=0)
    for r in range(out_ref.shape[0]):
        out_ref[r] = both


def eliminate(mats):
    sub8 = iota((8, LANES), 0)
    low = sub8 >= 4
    tiles = [[m[8 * t : 8 * t + 8] for t in range(4)] for m in mats]
    over = [[None] * 4 for _ in mats]
    wide = lambda x: jnp.broadcast_to(x, (8, LANES))
    for k in range(0, 32, 4):
        q, s = divmod(k, 8)
        for n, a in enumerate(tiles):
            r = [wide(a[q][s + i : s + i + 1, :]) for i in range(4)]
            cq = [jnp.maximum(wide(a[q][:, k + i : k + i + 1]), -jnp.inf) for i in range(4)]
            m = {(i, j): wide(cq[j][s + i : s + i + 1, :]) for i in range(4) for j in range(i, 4)}
            ia = 1.0 / (m[0, 0] * m[1, 1] - m[0, 1] * m[0, 1])
            x02 = (m[1, 1] * m[0, 2] - m[0, 1] * m[1, 2]) * ia
            x03 = (m[1, 1] * m[0, 3] - m[0, 1] * m[1, 3]) * ia
            x12 = (m[0, 0] * m[1, 2] - m[0, 1] * m[0, 2]) * ia
            x13 = (m[0, 0] * m[1, 3] - m[0, 1] * m[0, 3]) * ia
            s22 = m[2, 2] - m[0, 2] * x02 - m[1, 2] * x12
            s23 = m[2, 3] - m[0, 2] * x03 - m[1, 2] * x13
            s33 = m[3, 3] - m[0, 3] * x03 - m[1, 3] * x13
            ib = 1.0 / (s22 * s33 - s23 * s23)
            t0 = (m[1, 1] * r[0] - m[0, 1] * r[1]) * ia
            t1 = (m[0, 0] * r[1] - m[0, 1] * r[0]) * ia
            z2 = r[2] - x02 * r[0] - x12 * r[1]
            z3 = r[3] - x03 * r[0] - x13 * r[1]
            v2 = (s33 * z2 - s23 * z3) * ib
            v3 = (s22 * z3 - s23 * z2) * ib
            v0 = t0 - x02 * v2 - x03 * v3
            v1 = t1 - x12 * v2 - x13 * v3
            v = (v0, v1, v2, v3)
            got = v0
            for i in (1, 2, 3):
                got = jnp.where(sub8 >= s + i, v[i], got)
            over[n][q] = got if s == 0 else jnp.where(low, got, over[n][q])
            for t in range(q, 4):
                if t == q and s == 4:
                    continue
                c = cq if t == q else [wide(a[t][:, k + i : k + i + 1]) for i in range(4)]
                delta = (c[0] * v0 + c[1] * v1) + (c[2] * v2 + c[3] * v3)
                if t == q:
                    delta = jnp.where(low, delta, 0.0)
                a[t] = a[t] - delta
    u = [jnp.concatenate(a, axis=0) for a in tiles]
    v = [jnp.concatenate(a, axis=0) for a in over]
    return u, v


def finish_factor(u):
    sub8 = iota((8, LANES), 0)
    low = sub8 < 4
    within = sub8 & 3
    wide = lambda x: jnp.broadcast_to(x, (8, LANES))
    out = []
    for t in range(4):
        a = u[8 * t : 8 * t + 8]
        scale = jnp.zeros((8, LANES), F32)
        for i in range(4):
            row = jnp.where(low, wide(a[i : i + 1]), wide(a[4 + i : 5 + i]))
            at = 8 * t + i
            pivot = jnp.where(low, wide(row[:, at : at + 1]), wide(row[:, at + 4 : at + 5]))
            inv = 1.0 / pivot
            scale = jnp.where(within == i, jnp.sqrt(inv), scale)
            if i < 3:
                col = jnp.where(low, wide(a[:, at : at + 1]), wide(a[:, at + 4 : at + 5]))
                a = a - jnp.where(within > i, col * (row * inv), 0.0)
        out.append(a * scale)
    return jnp.concatenate(out, axis=0)


def tn_high(a, b):
    return nn_high(jnp.transpose(a), b)


def setup_kernel(recv_ref, probe_ref, small_ref):
    lane = iota((32, LANES), 1)
    gram = jnp.zeros((32, LANES), F32)
    for i in range(16):
        slab = recv_ref[:, i, :]
        moved = pltpu.roll(slab, (8 * i - 112) % LANES, 1)
        gram = jnp.where((lane >> 3) == i, moved, gram)
    gram = jnp.concatenate([gram[:, :64], gram[:, 64:]], axis=0)
    scaled = probe_ref[0:32]
    half = nn_high(scaled, gram)
    core = lax.dot_general(
        half, scaled, (((1,), (1,)), ((), ())), precision=HIGHEST, preferred_element_type=F32
    )
    eye = (iota((32, 32), 0) == iota((32, 32), 1)).astype(F32)
    zero64 = jnp.zeros((32, 64), F32)
    (u,), _ = eliminate([jnp.concatenate([core, eye, zero64], axis=1)])
    linv = finish_factor(u)[:, 32:64]
    projected = nn_high(linv, half)
    prior = lax.dot_general(
        projected * probe_ref[32:33],
        projected,
        (((1,), (1,)), ((), ())),
        precision=HIGHEST,
        preferred_element_type=F32,
    )
    (u,), (v,) = eliminate([jnp.concatenate([prior, eye, zero64], axis=1)])
    prec = tn_high(v[:, 32:64], u[:, 32:64])
    prec = 0.5 * (prec + jnp.transpose(prec))
    small_ref[...] = jnp.concatenate([linv, prec, zero64], axis=1)


def solve_kernel(recv_ref, small_ref, fp_ref, mean_hbm, spread_hbm, e_s, x_s, b_s, mean_ref, spread_ref, sems):
    lane = iota((32, LANES), 1)
    linv, prec = small_ref[:, :32], small_ref[:, 32:64]
    cells = fp_ref.shape[1]
    step = 1024
    one, two = halves(linv)
    onto = jnp.concatenate([one, one, two], axis=1).astype(BF16)
    for c in range(0, cells, step):
        basis = jnp.dot(onto, fp_ref[:, c : c + step], preferred_element_type=F32)
        top = basis.astype(BF16)
        b_s[0:32, c : c + step] = top
        b_s[32:64, c : c + step] = (basis - top.astype(F32)).astype(BF16)
        b_s[64:96, c : c + step] = top
    lt = jnp.transpose(linv)
    zero32 = jnp.zeros((32, 32), F32)
    eye = (iota((32, 32), 0) == iota((32, 32), 1)).astype(F32)
    k3 = jnp.concatenate([prec, prec, prec, zero32], axis=1)
    per_day = jnp.concatenate(
        [
            jnp.concatenate([x if i == j else zero32 for j in range(4)], axis=1)
            for i, x in enumerate((lt, lt, lt, eye))
        ],
        axis=0,
    )
    r16, c16 = iota((16, 16), 0), iota((16, 16), 1)
    zero_row = jnp.zeros((1, LANES), F32)
    dcols = []
    for r in range(8):
        x = recv_ref[r, :16, :]
        xt = jnp.transpose(x)
        slabs = []
        for d in range(3):
            a = x[:, 32 * d : 32 * d + 16]
            q = x[:, 32 * d + 16 : 32 * d + 32]
            at = xt[32 * d : 32 * d + 16]
            qt = xt[32 * d + 16 : 32 * d + 32]
            p = jnp.where(r16 <= c16, a, at)
            low = jnp.where(r16 == c16, x[:, 102 + d : 103 + d], jnp.where(r16 > c16, a, at))
            slabs.append(
                jnp.concatenate(
                    [jnp.concatenate([p, q], axis=1), jnp.concatenate([qt, low], axis=1)], axis=0
                )
            )
            dcols.append(
                jnp.concatenate(
                    [x[:, 105 + 2 * d : 106 + 2 * d], x[:, 106 + 2 * d : 107 + 2 * d]], axis=0
                )
            )
        gs = [
            jnp.concatenate([x[:, 96 + 2 * d : 97 + 2 * d], x[:, 97 + 2 * d : 98 + 2 * d]], axis=0)
            for d in range(3)
        ]
        x_s[:, r * LANES : (r + 1) * LANES] = jnp.concatenate(
            slabs + gs + [jnp.zeros((32, 29), F32)], axis=1
        )
    z = nn_high(linv, x_s[...])
    zs = jnp.concatenate([z[:, r * LANES : (r + 1) * LANES] for r in range(8)], axis=0)
    hs = nn_high(zs, per_day)
    first = [recv_ref[b // 3, 16 + b % 3 : 17 + b % 3, :] for b in range(24)]
    first.append(jnp.where(iota((1, LANES), 1) < 32, 1.0, 0.0))
    second = [recv_ref[b // 3, 19 + b % 3 : 20 + b % 3, :] for b in range(24)] + [zero_row]
    dcols.append(jnp.zeros((32, 1), F32))
    for b in range(25):
        nxt = (b + 1) % 25
        e = k3 * first[b] + (k3 * dcols[nxt]) * second[nxt]
        if b < 24:
            h = hs[32 * (b // 3) : 32 * (b // 3) + 32]
            d = b % 3
            mat = h if d == 0 else pltpu.roll(h, LANES - 32 * d, 1)
            vec = h if d == 0 else pltpu.roll(h, LANES - d, 1)
            e = e + jnp.where(lane < 32, mat, jnp.where(lane == 96, vec, 0.0))
        e_s[b] = e
    start = 3 * lax.axis_index("tm")
    nodes = [e_s[lax.rem(start + j, 25)] for j in range(25)]

    plan = [
        {0: [1, 3, 5, 7, 9, 11, 13, 15, 17, 19, 21, 23], 1: [2, 6, 10, 14, 18, 22], 2: [4, 12, 20], 3: [8, 24], 4: [16]},
        {0: [3, 5, 7, 9, 11, 13, 15, 17, 19, 21, 23], 1: [2, 6, 10, 14, 18, 22, 0], 2: [4, 12, 20], 3: [8, 24], 4: [16]},
        {0: [3, 5, 7, 9, 11, 13, 15, 17, 19, 21, 23, 1], 1: [6, 10, 14, 18, 22, 0], 2: [4, 12, 20], 3: [8, 24], 4: [16]},
    ]
    rings = [[(j, j) for j in range(25)] for _ in range(3)]
    values = dict(enumerate(nodes))
    fresh = [25]
    updated = {}

    def renew(key, make):
        if key not in updated:
            values[fresh[0]] = make()
            updated[key] = fresh[0]
            fresh[0] += 1
        return updated[key]

    for level in range(5):
        todo = []
        for target in range(3):
            held = dict(rings[target])
            todo += [held[j] for j in plan[target][level] if held[j] not in todo]
        us, vs = eliminate([values[i] for i in todo])
        prods = {}
        for i, u, v in zip(todo, us, vs):
            prods[i] = nn_high(jnp.transpose(v)[32:96], u)
        for target in range(3):
            ring = rings[target]
            gone = plan[target][level]
            size = len(ring)
            out = []
            for at, (j, i) in enumerate(ring):
                if j in gone:
                    continue
                pj, pi = ring[at - 1]
                nj, ni = ring[(at + 1) % size]
                key = i
                if nj in gone:
                    def as_left(i=i, ni=ni):
                        p = prods[ni][:32]
                        own = jnp.where(lane < 32, pltpu.roll(p, LANES - 32, 1), jnp.where(lane >= 64, p, 0.0))
                        kept = jnp.where((lane < 64) | (lane >= 96), values[i], 0.0)
                        return kept - own

                    i = renew(("l", i, ni), as_left)
                if pj in gone:
                    def as_right(i=i, pi=pi):
                        p = prods[pi][32:]
                        own = jnp.where(
                            lane < 32,
                            pltpu.roll(p, LANES - 64, 1),
                            jnp.where((lane < 64) | (lane >= 96), p, 0.0),
                        )
                        kept = jnp.where((lane < 32) | (lane >= 64), values[i], 0.0)
                        return kept - own

                    i = renew(("r", i, pi), as_right)
                out.append((j, i))
            rings[target] = out
    eye_at = jnp.where(lane == iota((32, LANES), 0) + 32, 1.0, 0.0)
    last = []
    for target in range(3):
        (pair,) = rings[target]
        m = values[pair[1]]
        m = m + jnp.where(lane < 32, pltpu.roll(m, LANES - 32, 1) + pltpu.roll(m, LANES - 64, 1), 0.0)
        last.append(jnp.where((lane < 32) | (lane >= 96), m, 0.0) + eye_at)
    us, vs = eliminate(last)
    rows, sums = [], []
    for u, v in zip(us, vs):
        vt = jnp.transpose(v)
        cov = nn_high(vt[32:64], u)[:, 32:64]
        rows.append(cov)
        sums.append(nn_high(vt[96:104], u)[0:1, 32:64])
    lhs = jnp.concatenate(rows + sums + [jnp.zeros((5, 32), F32)], axis=0)
    one, two = halves(lhs)
    lhs = jnp.concatenate([one, one, two], axis=1).astype(BF16)
    copies = []
    for part in range(2):
        half = slice(part * cells // 2, (part + 1) * cells // 2)
        for c in range(half.start, half.stop, step):
            b = b_s[:, c : c + step]
            y = jnp.dot(lhs, b, preferred_element_type=F32)
            wide = b[0:32].astype(F32) + b[32:64].astype(F32)
            for d in range(3):
                spread_ref[d : d + 1, c : c + step] = jnp.sum(
                    y[32 * d : 32 * d + 32] * wide, axis=0, keepdims=True
                )
            mean_ref[:, c : c + step] = y[96:99]
        for k, (ref, hbm) in enumerate(((mean_ref, mean_hbm), (spread_ref, spread_hbm))):
            copies.append(pltpu.make_async_copy(ref.at[:, half], hbm.at[:, half], sems.at[part, k]))
            copies[-1].start()
    for copy in copies:
        copy.wait()


def shape(*dims, dtype=F32):
    return jax.ShapeDtypeStruct(dims, dtype)


def on_chip(*xs):
    return tuple(pltpu.with_memory_space_constraint(x, pltpu.VMEM) for x in xs)


def call(kernel, out, scratch=(), in_specs=None, name=None, out_specs=None):
    extra = {} if in_specs is None else {"in_specs": in_specs}
    if out_specs is not None:
        extra["out_specs"] = out_specs
    return pl.pallas_call(
        kernel, out_shape=out, scratch_shapes=list(scratch), compiler_params=PARAMS, name=name, **extra
    )


VM = pl.BlockSpec(memory_space=pltpu.VMEM)
SM = pl.BlockSpec(memory_space=pltpu.SMEM)
ANY = pl.BlockSpec(memory_space=pl.ANY)


def body(
    background, probe, member_scale, decay, inflation, obs_owner, obs_offset, obs_value, obs_weight
):
    bt = background.T
    probe_t = probe.T
    scale = member_scale.reshape(1, -1)
    owner = obs_owner.transpose(0, 2, 1)
    cells = bt.shape[1]
    send = call(
        bucket_kernel,
        pltpu.VMEM((32, 1, 1280), F32),
        [
            pltpu.VMEM(bt.shape, BF16),
            pltpu.VMEM((3 * 16 * 32, 128), BF16),
            pltpu.VMEM((3, 192, 2048), BF16),
            pltpu.VMEM((3, 128, 2048), BF16),
            pltpu.SemaphoreType.DMA,
        ],
        in_specs=[VM, VM, VM, VM, ANY],
        name="buckets",
    )(owner, obs_offset, obs_value, obs_weight, bt)
    recv = lax.all_to_all(send, "space", 0, 0, tiled=True)
    ft, fp, scaled_probe, days = call(
        field_kernel,
        (
            pltpu.VMEM((32, cells), F32),
            pltpu.VMEM((96, cells), BF16),
            pltpu.VMEM((40, 64), F32),
            pltpu.VMEM((24, 128), F32),
        ),
        in_specs=[VM, VM, VM, VM, VM, SM],
        name="field",
    )(bt, probe_t, scale, decay, decay.T, inflation)
    recv, ft, fp, scaled_probe, days = on_chip(recv, ft, fp, scaled_probe, days)
    payload = call(
        gram_kernel,
        pltpu.VMEM((32, 16, 128), F32),
        [
            pltpu.VMEM((3, 256, 4096), BF16),
            pltpu.VMEM((3, 128, 4096), BF16),
            pltpu.VMEM((3, 64, 128), F32),
            pltpu.VMEM((3, 64, 128), F32),
            pltpu.VMEM((16, 128), F32),
        ],
        name="grams",
    )(recv, ft, fp)
    recv_2 = lax.all_to_all(payload, "space", 0, 0, tiled=True)
    (recv_2,) = on_chip(recv_2)
    both = call(total_kernel, pltpu.VMEM((8, 24, 128), F32), name="totals")(recv_2, days)
    recv_3 = lax.all_to_all(both, "tm", 0, 0, tiled=True)
    (recv_3,) = on_chip(recv_3)
    small = call(setup_kernel, pltpu.VMEM((32, 128), F32), name="setup")(recv_2, scaled_probe)
    (small,) = on_chip(small)
    mean, spread = call(
        solve_kernel,
        (shape(3, cells), shape(3, cells)),
        [
            pltpu.VMEM((25, 32, 128), F32),
            pltpu.VMEM((32, 1024), F32),
            pltpu.VMEM((96, cells), BF16),
            pltpu.VMEM((3, cells), F32),
            pltpu.VMEM((3, cells), F32),
            pltpu.SemaphoreType.DMA((2, 2)),
        ],
        in_specs=[VM, VM, VM],
        out_specs=(ANY, ANY),
        name="solve",
    )(recv_3, small, fp)
    return mean, spread


def solution(mesh):
    return jax.shard_map(
        body,
        mesh=mesh,
        in_specs=(
            P("space", None),
            P(),
            P(),
            P("tm", None),
            P("tm"),
            P("tm", "space", None),
            P("tm", "space"),
            P("tm", "space"),
            P("tm", "space"),
        ),
        out_specs=(P("tm", "space"), P("tm", "space")),
        check_vma=False,
    )
```

```python
import jax
import jax.numpy as jnp
from jax import lax
from jax.experimental import pallas as pl
from jax.experimental.pallas import tpu as pltpu
from jax.sharding import PartitionSpec as P

F32, BF16, I32 = jnp.float32, jnp.bfloat16, jnp.int32
HIGHEST = lax.Precision.HIGHEST
RANK = 32
LANES = 128
PARAMS = pltpu.CompilerParams(vmem_limit_bytes=56 << 20)


def iota(shape, dim):
    return lax.broadcasted_iota(I32, shape, dim)


def nt(a, b):
    return lax.dot_general(a, b, (((1,), (1,)), ((), ())), preferred_element_type=F32)


def nn_high(a, b):
    return lax.dot_general(
        a, b, (((1,), (0,)), ((), ())), precision=HIGHEST, preferred_element_type=F32
    )


def halves(x):
    top = x.astype(BF16).astype(F32)
    return top, x - top


def thirds(x):
    parts = []
    for _ in range(3):
        parts.append(x.astype(BF16))
        x = x - parts[-1].astype(F32)
    return parts


def packed(line, rows):
    line = jnp.broadcast_to(line, (16, LANES)).astype(BF16)
    return jnp.concatenate([line] * (rows // 16), axis=0)


def counter16(rows):
    return iota((rows, LANES), 0).astype(F32).astype(BF16)


def bucket_kernel(owner_ref, off_ref, val_ref, wgt_ref, bt_hbm, send_ref, bt_ref, oh_s, sem):
    fetch = pltpu.make_async_copy(bt_hbm, bt_ref, sem)
    fetch.start()
    days, _, obs = owner_ref.shape
    owners = send_ref.shape[0]
    chunks = obs // LANES
    upper = (iota((LANES, LANES), 0) < iota((LANES, LANES), 1)).astype(F32)
    counter = jnp.concatenate([upper, jnp.ones((LANES, LANES), F32)], axis=1).astype(BF16)
    sub_owner = counter16(owners)
    sub_slot = counter16(LANES)
    one, zero = jnp.ones((), BF16), jnp.zeros((), BF16)
    for d in range(days):
        for c in range(chunks):
            at = slice(c * LANES, (c + 1) * LANES)
            k = (d * chunks + c) * owners
            hit = sub_owner == packed(owner_ref[d, :, at].astype(F32), owners)
            oh_s[k : k + owners] = jnp.where(hit, one, zero)
    counts = jnp.dot(oh_s[...], counter, preferred_element_type=F32)
    for d in range(days):
        base = jnp.zeros((owners, LANES), F32)
        got = jnp.zeros((6 * owners, LANES), F32)
        for begin in range(0, chunks, 4):
            lefts, rights = [], []
            for c in range(begin, begin + 4):
                at = slice(c * LANES, (c + 1) * LANES)
                k = (d * chunks + c) * owners
                one_hot = oh_s[k : k + owners]
                count = counts[k : k + owners]
                slot = jnp.sum(
                    one_hot.astype(F32) * (count[:, :LANES] + base), axis=0, keepdims=True
                )
                base = base + count[:, LANES:]
                rights.append(jnp.where(sub_slot == packed(slot, LANES), one, zero))
                weight = wgt_ref[d : d + 1, at]
                offset = off_ref[d : d + 1, at]
                fields = (
                    *halves(weight),
                    *halves(weight * val_ref[d : d + 1, at]),
                    (offset >> 7).astype(F32),
                    (offset & 127).astype(F32),
                )
                lefts.append(
                    jnp.concatenate([one_hot * packed(row, owners) for row in fields], axis=0)
                )
            got = got + nt(jnp.concatenate(lefts, axis=1), jnp.concatenate(rights, axis=1))
        part = [got[f * owners : (f + 1) * owners] for f in range(6)]
        for f, x in enumerate((part[0] + part[1], part[2] + part[3], part[4] * 128.0 + part[5])):
            j = f * days + d
            send_ref[:, 0, j * LANES : (j + 1) * LANES] = x
    fetch.wait()
    gram = nt(bt_ref[...], bt_ref[...])
    send_ref[:, 0, 9 * LANES : 10 * LANES] = jnp.concatenate([gram[:32], gram[32:]], axis=1)


def field_kernel(
    bt_ref, probe_ref, scale_ref, decay_ref, decay_t_ref, infl_ref, ft_ref, fp_ref, probe_out, days_ref
):
    scale = scale_ref[...]
    scaled = (probe_ref[...].astype(F32) * scale).astype(BF16)
    ft = jnp.dot(scaled, bt_ref[...], preferred_element_type=F32)
    ft_ref[...] = ft
    top = ft.astype(BF16)
    fp_ref[0:32] = top
    fp_ref[32:64] = (ft - top.astype(F32)).astype(BF16)
    fp_ref[64:96] = top
    probe_out[0:32] = scaled.astype(F32)
    probe_out[32:40] = jnp.broadcast_to(scale * scale, (8, scale.shape[1]))
    lane16, lane1 = iota((16, LANES), 1), iota((1, LANES), 1)
    columns = jnp.zeros((16, LANES), F32)
    first, second = [], []
    for d in range(3):
        columns = jnp.where(lane16 == 105 + d, decay_t_ref[:16, d : d + 1], columns)
        columns = jnp.where(lane16 == 108 + d, decay_t_ref[16:, d : d + 1], columns)
        gamma = 1.0 / infl_ref[d]
        decay = jnp.concatenate([decay_ref[d : d + 1, :]] * 4, axis=1)
        right = (lane1 >= 64) & (lane1 < 96)
        first.append(jnp.where(lane1 < 32, gamma, jnp.where(lane1 < 64, -gamma * decay, 0.0)))
        second.append(jnp.where(lane1 < 32, gamma * decay, jnp.where(right, -gamma, 0.0)))
    rows = first + second + [jnp.zeros((2, LANES), F32)]
    days_ref[...] = jnp.concatenate([columns] + rows, axis=0)


def gram_kernel(recv_ref, ft_ref, fp_ref, out_ref, wc_s, uc_s, pay_s):
    readers = recv_ref.shape[0]
    days = 3
    sub64, sub128 = counter16(64), counter16(LANES)
    one, zero = jnp.ones((), BF16), jnp.zeros((), BF16)

    for d in range(days):
        w = halves(recv_ref[:, 0, d * LANES : (d + 1) * LANES])
        u = halves(recv_ref[:, 0, (3 + d) * LANES : (4 + d) * LANES])
        offset = recv_ref[:, 0, (6 + d) * LANES : (7 + d) * LANES].astype(I32)
        high, low = (offset >> 7).astype(F32), (offset & 127).astype(F32)
        got = jnp.zeros((256, LANES), F32)
        for begin in range(0, readers, 4):
            lefts, rights = [], []
            for r in range(begin, begin + 4):
                hit = sub64 == packed(high[r : r + 1], 64)
                lefts.append(
                    jnp.concatenate(
                        [jnp.where(hit, packed(x[r : r + 1], 64), zero) for x in w + u], axis=0
                    )
                )
                rights.append(jnp.where(sub128 == packed(low[r : r + 1], LANES), one, zero))
            got = got + nt(jnp.concatenate(lefts, axis=1), jnp.concatenate(rights, axis=1))
        wc_s[d] = got[:64] + got[64:128]
        uc_s[d] = got[128:192] + got[192:]
    accs = [jnp.zeros((RANK, LANES), F32)] * days
    prod = jnp.zeros((days * 64, 64), F32)
    for start in range(0, 64, 4):
        xs = []
        for h in range(start, start + 4):
            ft = ft_ref[:, h * LANES : (h + 1) * LANES]
            pieces = []
            for d in range(days):
                x = ft * wc_s[d, h : h + 1, :]
                top = x.astype(BF16)
                pieces += [top, (x - top.astype(F32)).astype(BF16)]
                accs[d] = accs[d] + ft * uc_s[d, h : h + 1, :]
            xs.append(jnp.concatenate(pieces, axis=0))
        x = jnp.concatenate(xs, axis=1)
        prod = prod + nt(x, fp_ref[0:64, start * LANES : (start + 4) * LANES])
    chunk = jnp.sum(recv_ref[:, 0, 9 * LANES : 10 * LANES], axis=0, keepdims=True)
    row16, lane16 = iota((16, LANES), 0), iota((16, LANES), 1)
    fold = jnp.where((lane16 >> 3) == row16, chunk, 0.0)
    for shift in (64, 32, 16, 8):
        fold = fold + pltpu.roll(fold, shift, 1)
    pay = jnp.where((lane16 >= 112) & (lane16 < 120), fold, 0.0)
    r16, c16 = iota((16, 16), 0), iota((16, 16), 1)
    pieces = []
    for d in range(days):
        p = prod[d * 64 : (d + 1) * 64]
        sym = p[:32, :32] + p[:32, 32:] + p[32:, :32] + p[32:, 32:]
        low = sym[16:, 16:]
        pieces += [jnp.where(r16 <= c16, sym[:16, :16], low), sym[:16, 16:]]
        diag = jnp.sum(jnp.where(r16 == c16, low, 0.0), axis=1, keepdims=True)
        g = jnp.sum(accs[d], axis=1, keepdims=True)
        pay = jnp.where(lane16 == 96 + d, g[:16], pay)
        pay = jnp.where(lane16 == 99 + d, g[16:], pay)
        pay = jnp.where(lane16 == 102 + d, diag, pay)
    pay_s[...] = pay
    for k, piece in enumerate(pieces):
        pay_s[:, 16 * k : 16 * (k + 1)] = piece
    pay = pay_s[...]
    for r in range(readers):
        out_ref[r] = pay


def total_kernel(recv_ref, days_ref, out_ref):
    total = jnp.sum(recv_ref[...], axis=0)
    both = days_ref[...] + jnp.concatenate([total, jnp.zeros((8, LANES), F32)], axis=0)
    for r in range(out_ref.shape[0]):
        out_ref[r] = both


def eliminate(mats):
    sub8 = iota((8, LANES), 0)
    low = sub8 >= 4
    tiles = [[m[8 * t : 8 * t + 8] for t in range(4)] for m in mats]
    over = [[None] * 4 for _ in mats]
    wide = lambda x: jnp.broadcast_to(x, (8, LANES))
    for k in range(0, 32, 4):
        q, s = divmod(k, 8)
        for n, a in enumerate(tiles):
            r = [wide(a[q][s + i : s + i + 1, :]) for i in range(4)]
            cq = [jnp.maximum(wide(a[q][:, k + i : k + i + 1]), -jnp.inf) for i in range(4)]
            m = {(i, j): wide(cq[j][s + i : s + i + 1, :]) for i in range(4) for j in range(i, 4)}
            ia = 1.0 / (m[0, 0] * m[1, 1] - m[0, 1] * m[0, 1])
            x02 = (m[1, 1] * m[0, 2] - m[0, 1] * m[1, 2]) * ia
            x03 = (m[1, 1] * m[0, 3] - m[0, 1] * m[1, 3]) * ia
            x12 = (m[0, 0] * m[1, 2] - m[0, 1] * m[0, 2]) * ia
            x13 = (m[0, 0] * m[1, 3] - m[0, 1] * m[0, 3]) * ia
            s22 = m[2, 2] - m[0, 2] * x02 - m[1, 2] * x12
            s23 = m[2, 3] - m[0, 2] * x03 - m[1, 2] * x13
            s33 = m[3, 3] - m[0, 3] * x03 - m[1, 3] * x13
            ib = 1.0 / (s22 * s33 - s23 * s23)
            t0 = (m[1, 1] * r[0] - m[0, 1] * r[1]) * ia
            t1 = (m[0, 0] * r[1] - m[0, 1] * r[0]) * ia
            z2 = r[2] - x02 * r[0] - x12 * r[1]
            z3 = r[3] - x03 * r[0] - x13 * r[1]
            v2 = (s33 * z2 - s23 * z3) * ib
            v3 = (s22 * z3 - s23 * z2) * ib
            v0 = t0 - x02 * v2 - x03 * v3
            v1 = t1 - x12 * v2 - x13 * v3
            v = (v0, v1, v2, v3)
            got = v0
            for i in (1, 2, 3):
                got = jnp.where(sub8 >= s + i, v[i], got)
            over[n][q] = got if s == 0 else jnp.where(low, got, over[n][q])
            for t in range(q, 4):
                if t == q and s == 4:
                    continue
                c = cq if t == q else [wide(a[t][:, k + i : k + i + 1]) for i in range(4)]
                delta = (c[0] * v0 + c[1] * v1) + (c[2] * v2 + c[3] * v3)
                if t == q:
                    delta = jnp.where(low, delta, 0.0)
                a[t] = a[t] - delta
    u = [jnp.concatenate(a, axis=0) for a in tiles]
    v = [jnp.concatenate(a, axis=0) for a in over]
    return u, v


def finish_factor(u):
    sub8 = iota((8, LANES), 0)
    low = sub8 < 4
    within = sub8 & 3
    wide = lambda x: jnp.broadcast_to(x, (8, LANES))
    out = []
    for t in range(4):
        a = u[8 * t : 8 * t + 8]
        scale = jnp.zeros((8, LANES), F32)
        for i in range(4):
            row = jnp.where(low, wide(a[i : i + 1]), wide(a[4 + i : 5 + i]))
            at = 8 * t + i
            pivot = jnp.where(low, wide(row[:, at : at + 1]), wide(row[:, at + 4 : at + 5]))
            inv = 1.0 / pivot
            scale = jnp.where(within == i, jnp.sqrt(inv), scale)
            if i < 3:
                col = jnp.where(low, wide(a[:, at : at + 1]), wide(a[:, at + 4 : at + 5]))
                a = a - jnp.where(within > i, col * (row * inv), 0.0)
        out.append(a * scale)
    return jnp.concatenate(out, axis=0)


def tn_high(a, b):
    return nn_high(jnp.transpose(a), b)


def setup_kernel(recv_ref, probe_ref, small_ref):
    lane = iota((32, LANES), 1)
    gram = jnp.zeros((32, LANES), F32)
    for i in range(16):
        slab = recv_ref[:, i, :]
        moved = pltpu.roll(slab, (8 * i - 112) % LANES, 1)
        gram = jnp.where((lane >> 3) == i, moved, gram)
    gram = jnp.concatenate([gram[:, :64], gram[:, 64:]], axis=0)
    scaled = probe_ref[0:32]
    half = nn_high(scaled, gram)
    core = lax.dot_general(
        half, scaled, (((1,), (1,)), ((), ())), precision=HIGHEST, preferred_element_type=F32
    )
    eye = (iota((32, 32), 0) == iota((32, 32), 1)).astype(F32)
    zero64 = jnp.zeros((32, 64), F32)
    (u,), _ = eliminate([jnp.concatenate([core, eye, zero64], axis=1)])
    linv = finish_factor(u)[:, 32:64]
    projected = nn_high(linv, half)
    prior = lax.dot_general(
        projected * probe_ref[32:33],
        projected,
        (((1,), (1,)), ((), ())),
        precision=HIGHEST,
        preferred_element_type=F32,
    )
    (u,), (v,) = eliminate([jnp.concatenate([prior, eye, zero64], axis=1)])
    prec = tn_high(v[:, 32:64], u[:, 32:64])
    prec = 0.5 * (prec + jnp.transpose(prec))
    small_ref[...] = jnp.concatenate([linv, prec, zero64], axis=1)


def unfold(x, roll):
    row, lane = iota((16, LANES), 0), iota((16, LANES), 1)
    col = lane & 15
    turned = jnp.transpose(x)
    turned = jnp.concatenate([turned[16 * b : 16 * b + 16] for b in range(8)], axis=1)
    top = jnp.where((lane < 96) & ((lane & 16) == 0) & (row > col), turned, x)
    diag = jnp.zeros((16, LANES), F32)
    for d in range(3):
        diag = jnp.where((lane >> 5) == d, x[:, 102 + d : 103 + d], diag)
    corner = roll(jnp.where(row > col, x, turned), 16, 1)
    corner = jnp.where(row == col, diag, corner)
    low = jnp.where((lane & 16) == 0, roll(turned, LANES - 16, 1), corner)
    low = jnp.where(lane < 96, low, roll(x, LANES - 3, 1))
    both = jnp.concatenate([top, low], axis=0)
    return jnp.where(iota((32, LANES), 1) < 99, both, 0.0)


def solve_kernel(recv_ref, small_ref, fp_ref, mean_hbm, spread_hbm, e_s, x_s, b_s, mean_ref, spread_ref, sems):
    lane = iota((32, LANES), 1)
    linv, prec = small_ref[:, :32], small_ref[:, 32:64]
    cells = fp_ref.shape[1]
    step = 1024
    one, two = halves(linv)
    onto = jnp.concatenate([one, one, two], axis=1).astype(BF16)
    for c in range(0, cells, step):
        basis = jnp.dot(onto, fp_ref[:, c : c + step], preferred_element_type=F32)
        top = basis.astype(BF16)
        b_s[0:32, c : c + step] = top
        b_s[32:64, c : c + step] = (basis - top.astype(F32)).astype(BF16)
        b_s[64:96, c : c + step] = top
    lt = jnp.transpose(linv)
    zero32 = jnp.zeros((32, 32), F32)
    eye = (iota((32, 32), 0) == iota((32, 32), 1)).astype(F32)
    k3 = jnp.concatenate([prec, prec, prec, zero32], axis=1)
    per_day = jnp.concatenate(
        [
            jnp.concatenate([x if i == j else zero32 for j in range(4)], axis=1)
            for i, x in enumerate((lt, lt, lt, eye))
        ],
        axis=0,
    )
    zero_row = jnp.zeros((1, LANES), F32)
    dcols = []
    for r in range(8):
        x = recv_ref[r, :16, :]
        x_s[:, r * LANES : (r + 1) * LANES] = unfold(x, pltpu.roll)
        for d in range(3):
            column = (x[:, 105 + d : 106 + d], x[:, 108 + d : 109 + d])
            dcols.append(jnp.concatenate(column, axis=0))
    z = nn_high(linv, x_s[...])
    zs = jnp.concatenate([z[:, r * LANES : (r + 1) * LANES] for r in range(8)], axis=0)
    hs = nn_high(zs, per_day)
    first = [recv_ref[b // 3, 16 + b % 3 : 17 + b % 3, :] for b in range(24)]
    first.append(jnp.where(iota((1, LANES), 1) < 32, 1.0, 0.0))
    second = [recv_ref[b // 3, 19 + b % 3 : 20 + b % 3, :] for b in range(24)] + [zero_row]
    dcols.append(jnp.zeros((32, 1), F32))
    for b in range(25):
        nxt = (b + 1) % 25
        e = k3 * first[b] + (k3 * dcols[nxt]) * second[nxt]
        if b < 24:
            h = hs[32 * (b // 3) : 32 * (b // 3) + 32]
            d = b % 3
            mat = h if d == 0 else pltpu.roll(h, LANES - 32 * d, 1)
            vec = h if d == 0 else pltpu.roll(h, LANES - d, 1)
            e = e + jnp.where(lane < 32, mat, jnp.where(lane == 96, vec, 0.0))
        e_s[b] = e
    start = 3 * lax.axis_index("tm")
    nodes = [e_s[lax.rem(start + j, 25)] for j in range(25)]

    plan = [
        {0: [1, 3, 5, 7, 9, 11, 13, 15, 17, 19, 21, 23], 1: [2, 6, 10, 14, 18, 22], 2: [4, 12, 20], 3: [8, 24], 4: [16]},
        {0: [3, 5, 7, 9, 11, 13, 15, 17, 19, 21, 23], 1: [2, 6, 10, 14, 18, 22, 0], 2: [4, 12, 20], 3: [8, 24], 4: [16]},
        {0: [3, 5, 7, 9, 11, 13, 15, 17, 19, 21, 23, 1], 1: [6, 10, 14, 18, 22, 0], 2: [4, 12, 20], 3: [8, 24], 4: [16]},
    ]
    rings = [[(j, j) for j in range(25)] for _ in range(3)]
    values = dict(enumerate(nodes))
    fresh = [25]
    updated = {}

    def renew(key, make):
        if key not in updated:
            values[fresh[0]] = make()
            updated[key] = fresh[0]
            fresh[0] += 1
        return updated[key]

    for level in range(5):
        todo = []
        for target in range(3):
            held = dict(rings[target])
            todo += [held[j] for j in plan[target][level] if held[j] not in todo]
        us, vs = eliminate([values[i] for i in todo])
        prods = {}
        for i, u, v in zip(todo, us, vs):
            prods[i] = nn_high(jnp.transpose(v)[32:96], u)
        for target in range(3):
            ring = rings[target]
            gone = plan[target][level]
            size = len(ring)
            out = []
            for at, (j, i) in enumerate(ring):
                if j in gone:
                    continue
                pj, pi = ring[at - 1]
                nj, ni = ring[(at + 1) % size]
                key = i
                if nj in gone:
                    def as_left(i=i, ni=ni):
                        p = prods[ni][:32]
                        own = jnp.where(lane < 32, pltpu.roll(p, LANES - 32, 1), jnp.where(lane >= 64, p, 0.0))
                        kept = jnp.where((lane < 64) | (lane >= 96), values[i], 0.0)
                        return kept - own

                    i = renew(("l", i, ni), as_left)
                if pj in gone:
                    def as_right(i=i, pi=pi):
                        p = prods[pi][32:]
                        own = jnp.where(
                            lane < 32,
                            pltpu.roll(p, LANES - 64, 1),
                            jnp.where((lane < 64) | (lane >= 96), p, 0.0),
                        )
                        kept = jnp.where((lane < 32) | (lane >= 64), values[i], 0.0)
                        return kept - own

                    i = renew(("r", i, pi), as_right)
                out.append((j, i))
            rings[target] = out
    eye_at = jnp.where(lane == iota((32, LANES), 0) + 32, 1.0, 0.0)
    last = []
    for target in range(3):
        (pair,) = rings[target]
        m = values[pair[1]]
        m = m + jnp.where(lane < 32, pltpu.roll(m, LANES - 32, 1) + pltpu.roll(m, LANES - 64, 1), 0.0)
        last.append(jnp.where((lane < 32) | (lane >= 96), m, 0.0) + eye_at)
    us, vs = eliminate(last)
    rows, sums = [], []
    for u, v in zip(us, vs):
        vt = jnp.transpose(v)
        cov = nn_high(vt[32:64], u)[:, 32:64]
        rows.append(cov)
        sums.append(nn_high(vt[96:104], u)[0:1, 32:64])
    lhs = jnp.concatenate(rows + sums + [jnp.zeros((5, 32), F32)], axis=0)
    one, two = halves(lhs)
    lhs = jnp.concatenate([one, one, two], axis=1).astype(BF16)
    copies = []
    for part in range(2):
        half = slice(part * cells // 2, (part + 1) * cells // 2)
        for c in range(half.start, half.stop, step):
            b = b_s[:, c : c + step]
            y = jnp.dot(lhs, b, preferred_element_type=F32)
            wide = b[0:32].astype(F32) + b[32:64].astype(F32)
            for d in range(3):
                spread_ref[d : d + 1, c : c + step] = jnp.sum(
                    y[32 * d : 32 * d + 32] * wide, axis=0, keepdims=True
                )
            mean_ref[:, c : c + step] = y[96:99]
        for k, (ref, hbm) in enumerate(((mean_ref, mean_hbm), (spread_ref, spread_hbm))):
            copies.append(pltpu.make_async_copy(ref.at[:, half], hbm.at[:, half], sems.at[part, k]))
            copies[-1].start()
    for copy in copies:
        copy.wait()


def shape(*dims, dtype=F32):
    return jax.ShapeDtypeStruct(dims, dtype)


def on_chip(*xs):
    return tuple(pltpu.with_memory_space_constraint(x, pltpu.VMEM) for x in xs)


def call(kernel, out, scratch=(), in_specs=None, name=None, out_specs=None):
    extra = {} if in_specs is None else {"in_specs": in_specs}
    if out_specs is not None:
        extra["out_specs"] = out_specs
    return pl.pallas_call(
        kernel, out_shape=out, scratch_shapes=list(scratch), compiler_params=PARAMS, name=name, **extra
    )


VM = pl.BlockSpec(memory_space=pltpu.VMEM)
SM = pl.BlockSpec(memory_space=pltpu.SMEM)
ANY = pl.BlockSpec(memory_space=pl.ANY)


def body(
    background, probe, member_scale, decay, inflation, obs_owner, obs_offset, obs_value, obs_weight
):
    bt = background.T
    probe_t = probe.T
    scale = member_scale.reshape(1, -1)
    owner = obs_owner.transpose(0, 2, 1)
    cells = bt.shape[1]
    send = call(
        bucket_kernel,
        pltpu.VMEM((32, 1, 1280), F32),
        [
            pltpu.VMEM(bt.shape, BF16),
            pltpu.VMEM((3 * 16 * 32, 128), BF16),
            pltpu.SemaphoreType.DMA,
        ],
        in_specs=[VM, VM, VM, VM, ANY],
        name="buckets",
    )(owner, obs_offset, obs_value, obs_weight, bt)
    recv = lax.all_to_all(send, "space", 0, 0, tiled=True)
    ft, fp, scaled_probe, days = call(
        field_kernel,
        (
            pltpu.VMEM((32, cells), F32),
            pltpu.VMEM((96, cells), BF16),
            pltpu.VMEM((40, 64), F32),
            pltpu.VMEM((24, 128), F32),
        ),
        in_specs=[VM, VM, VM, VM, VM, SM],
        name="field",
    )(bt, probe_t, scale, decay, decay.T, inflation)
    recv, ft, fp, scaled_probe, days = on_chip(recv, ft, fp, scaled_probe, days)
    payload = call(
        gram_kernel,
        pltpu.VMEM((32, 16, 128), F32),
        [
            pltpu.VMEM((3, 64, 128), F32),
            pltpu.VMEM((3, 64, 128), F32),
            pltpu.VMEM((16, 128), F32),
        ],
        name="grams",
    )(recv, ft, fp)
    recv_2 = lax.all_to_all(payload, "space", 0, 0, tiled=True)
    (recv_2,) = on_chip(recv_2)
    both = call(total_kernel, pltpu.VMEM((8, 24, 128), F32), name="totals")(recv_2, days)
    recv_3 = lax.all_to_all(both, "tm", 0, 0, tiled=True)
    (recv_3,) = on_chip(recv_3)
    small = call(setup_kernel, pltpu.VMEM((32, 128), F32), name="setup")(recv_2, scaled_probe)
    (small,) = on_chip(small)
    mean, spread = call(
        solve_kernel,
        (shape(3, cells), shape(3, cells)),
        [
            pltpu.VMEM((25, 32, 128), F32),
            pltpu.VMEM((32, 1024), F32),
            pltpu.VMEM((96, cells), BF16),
            pltpu.VMEM((3, cells), F32),
            pltpu.VMEM((3, cells), F32),
            pltpu.SemaphoreType.DMA((2, 2)),
        ],
        in_specs=[VM, VM, VM],
        out_specs=(ANY, ANY),
        name="solve",
    )(recv_3, small, fp)
    return mean, spread


def solution(mesh):
    return jax.shard_map(
        body,
        mesh=mesh,
        in_specs=(
            P("space", None),
            P(),
            P(),
            P("tm", None),
            P("tm"),
            P("tm", "space", None),
            P("tm", "space"),
            P("tm", "space"),
            P("tm", "space"),
        ),
        out_specs=(P("tm", "space"), P("tm", "space")),
        check_vma=False,
    )
```

```python
import jax
import jax.numpy as jnp
from jax import lax
from jax.experimental import pallas as pl
from jax.experimental.pallas import tpu as pltpu
from jax.sharding import PartitionSpec as P

F32, BF16, I32 = jnp.float32, jnp.bfloat16, jnp.int32
HIGHEST = lax.Precision.HIGHEST
RANK = 32
LANES = 128
PARAMS = pltpu.CompilerParams(vmem_limit_bytes=56 << 20)


def iota(shape, dim):
    return lax.broadcasted_iota(I32, shape, dim)


def nt(a, b):
    return lax.dot_general(a, b, (((1,), (1,)), ((), ())), preferred_element_type=F32)


def nn_high(a, b):
    return lax.dot_general(
        a, b, (((1,), (0,)), ((), ())), precision=HIGHEST, preferred_element_type=F32
    )


def halves(x):
    top = x.astype(BF16).astype(F32)
    return top, x - top


def thirds(x):
    parts = []
    for _ in range(3):
        parts.append(x.astype(BF16))
        x = x - parts[-1].astype(F32)
    return parts


def packed(line, rows):
    line = jnp.broadcast_to(line, (16, LANES)).astype(BF16)
    return jnp.concatenate([line] * (rows // 16), axis=0)


def counter16(rows):
    return iota((rows, LANES), 0).astype(F32).astype(BF16)


def bucket_kernel(owner_ref, off_ref, val_ref, wgt_ref, bt_hbm, send_ref, bt_ref, oh_s, sem):
    fetch = pltpu.make_async_copy(bt_hbm, bt_ref, sem)
    fetch.start()
    days, _, obs = owner_ref.shape
    owners = send_ref.shape[0]
    chunks = obs // LANES
    upper = (iota((LANES, LANES), 0) < iota((LANES, LANES), 1)).astype(F32)
    counter = jnp.concatenate([upper, jnp.ones((LANES, LANES), F32)], axis=1).astype(BF16)
    sub_owner = counter16(owners)
    sub_slot = counter16(LANES)
    one, zero = jnp.ones((), BF16), jnp.zeros((), BF16)
    for d in range(days):
        for c in range(chunks):
            at = slice(c * LANES, (c + 1) * LANES)
            k = (d * chunks + c) * owners
            hit = sub_owner == packed(owner_ref[d, :, at].astype(F32), owners)
            oh_s[k : k + owners] = jnp.where(hit, one, zero)
    counts = jnp.dot(oh_s[...], counter, preferred_element_type=F32)
    for d in range(days):
        base = jnp.zeros((owners, LANES), F32)
        got = jnp.zeros((6 * owners, LANES), F32)
        for begin in range(0, chunks, 4):
            lefts, rights = [], []
            for c in range(begin, begin + 4):
                at = slice(c * LANES, (c + 1) * LANES)
                k = (d * chunks + c) * owners
                one_hot = oh_s[k : k + owners]
                count = counts[k : k + owners]
                slot = jnp.sum(
                    one_hot.astype(F32) * (count[:, :LANES] + base), axis=0, keepdims=True
                )
                base = base + count[:, LANES:]
                rights.append(jnp.where(sub_slot == packed(slot, LANES), one, zero))
                weight = wgt_ref[d : d + 1, at]
                offset = off_ref[d : d + 1, at]
                fields = (
                    *halves(weight),
                    *halves(weight * val_ref[d : d + 1, at]),
                    (offset >> 7).astype(F32),
                    (offset & 127).astype(F32),
                )
                lefts.append(
                    jnp.concatenate([one_hot * packed(row, owners) for row in fields], axis=0)
                )
            got = got + nt(jnp.concatenate(lefts, axis=1), jnp.concatenate(rights, axis=1))
        part = [got[f * owners : (f + 1) * owners] for f in range(6)]
        for f, x in enumerate((part[0] + part[1], part[2] + part[3], part[4] * 128.0 + part[5])):
            j = f * days + d
            send_ref[:, 0, j * LANES : (j + 1) * LANES] = x
    fetch.wait()
    gram = nt(bt_ref[...], bt_ref[...])
    send_ref[:, 0, 9 * LANES : 10 * LANES] = jnp.concatenate([gram[:32], gram[32:]], axis=1)


def field_kernel(
    bt_ref, probe_ref, scale_ref, decay_ref, decay_t_ref, infl_ref, ft_ref, fp_ref, probe_out, days_ref
):
    scale = scale_ref[...]
    scaled = (probe_ref[...].astype(F32) * scale).astype(BF16)
    ft = jnp.dot(scaled, bt_ref[...], preferred_element_type=F32)
    ft_ref[...] = ft
    top = ft.astype(BF16)
    fp_ref[0:32] = top
    fp_ref[32:64] = (ft - top.astype(F32)).astype(BF16)
    fp_ref[64:96] = top
    probe_out[0:32] = scaled.astype(F32)
    probe_out[32:40] = jnp.broadcast_to(scale * scale, (8, scale.shape[1]))
    lane16, lane1 = iota((16, LANES), 1), iota((1, LANES), 1)
    columns = jnp.zeros((16, LANES), F32)
    first, second = [], []
    for d in range(3):
        columns = jnp.where(lane16 == 105 + d, decay_t_ref[:16, d : d + 1], columns)
        columns = jnp.where(lane16 == 108 + d, decay_t_ref[16:, d : d + 1], columns)
        gamma = 1.0 / infl_ref[d]
        decay = jnp.concatenate([decay_ref[d : d + 1, :]] * 4, axis=1)
        right = (lane1 >= 64) & (lane1 < 96)
        first.append(jnp.where(lane1 < 32, gamma, jnp.where(lane1 < 64, -gamma * decay, 0.0)))
        second.append(jnp.where(lane1 < 32, gamma * decay, jnp.where(right, -gamma, 0.0)))
    rows = first + second + [jnp.zeros((2, LANES), F32)]
    days_ref[...] = jnp.concatenate([columns] + rows, axis=0)


def gram_kernel(recv_ref, ft_ref, fp_ref, out_ref, wc_s, uc_s, pay_s):
    readers = recv_ref.shape[0]
    days = 3
    sub64, sub128 = counter16(64), counter16(LANES)
    one, zero = jnp.ones((), BF16), jnp.zeros((), BF16)

    def counting(d):
        w = halves(recv_ref[:, 0, d * LANES : (d + 1) * LANES])
        u = halves(recv_ref[:, 0, (3 + d) * LANES : (4 + d) * LANES])
        offset = recv_ref[:, 0, (6 + d) * LANES : (7 + d) * LANES].astype(I32)
        high, low = (offset >> 7).astype(F32), (offset & 127).astype(F32)
        got = jnp.zeros((256, LANES), F32)
        for begin in range(0, readers, 4):
            lefts, rights = [], []
            for r in range(begin, begin + 4):
                hit = sub64 == packed(high[r : r + 1], 64)
                lefts.append(
                    jnp.concatenate(
                        [jnp.where(hit, packed(x[r : r + 1], 64), zero) for x in w + u], axis=0
                    )
                )
                rights.append(jnp.where(sub128 == packed(low[r : r + 1], LANES), one, zero))
            got = got + nt(jnp.concatenate(lefts, axis=1), jnp.concatenate(rights, axis=1))
            yield
        wc_s[d] = got[:64] + got[64:128]
        uc_s[d] = got[128:192] + got[192:]

    accs, prods = [None] * days, [None] * days

    def weighing(d):
        acc, prod = jnp.zeros((RANK, LANES), F32), jnp.zeros((64, 64), F32)
        for start in range(0, 64, 4):
            xs = []
            for h in range(start, start + 4):
                ft = ft_ref[:, h * LANES : (h + 1) * LANES]
                x = ft * wc_s[d, h : h + 1, :]
                top = x.astype(BF16)
                xs.append(jnp.concatenate([top, (x - top.astype(F32)).astype(BF16)], axis=0))
                acc = acc + ft * uc_s[d, h : h + 1, :]
            x = jnp.concatenate(xs, axis=1)
            prod = prod + nt(x, fp_ref[0:64, start * LANES : (start + 4) * LANES])
            yield
        accs[d], prods[d] = acc, prod

    for d in range(days + 1):
        work = [counting(d)] if d < days else []
        work += [weighing(d - 1)] if d else []
        while work:
            work = [w for w in work if next(w, "done") != "done"]
    chunk = jnp.sum(recv_ref[:, 0, 9 * LANES : 10 * LANES], axis=0, keepdims=True)
    row16, lane16 = iota((16, LANES), 0), iota((16, LANES), 1)
    fold = jnp.where((lane16 >> 3) == row16, chunk, 0.0)
    for shift in (64, 32, 16, 8):
        fold = fold + pltpu.roll(fold, shift, 1)
    pay = jnp.where((lane16 >= 112) & (lane16 < 120), fold, 0.0)
    r16, c16 = iota((16, 16), 0), iota((16, 16), 1)
    pieces = []
    for d in range(days):
        p = prods[d]
        sym = p[:32, :32] + p[:32, 32:] + p[32:, :32] + p[32:, 32:]
        low = sym[16:, 16:]
        pieces += [jnp.where(r16 <= c16, sym[:16, :16], low), sym[:16, 16:]]
        diag = jnp.sum(jnp.where(r16 == c16, low, 0.0), axis=1, keepdims=True)
        g = jnp.sum(accs[d], axis=1, keepdims=True)
        pay = jnp.where(lane16 == 96 + d, g[:16], pay)
        pay = jnp.where(lane16 == 99 + d, g[16:], pay)
        pay = jnp.where(lane16 == 102 + d, diag, pay)
    pay_s[...] = pay
    for k, piece in enumerate(pieces):
        pay_s[:, 16 * k : 16 * (k + 1)] = piece
    pay = pay_s[...]
    for r in range(readers):
        out_ref[r] = pay


def total_kernel(recv_ref, days_ref, out_ref):
    total = jnp.sum(recv_ref[...], axis=0)
    both = days_ref[...] + jnp.concatenate([total, jnp.zeros((8, LANES), F32)], axis=0)
    for r in range(out_ref.shape[0]):
        out_ref[r] = both


def eliminate(mats):
    sub8 = iota((8, LANES), 0)
    low = sub8 >= 4
    tiles = [[m[8 * t : 8 * t + 8] for t in range(4)] for m in mats]
    over = [[None] * 4 for _ in mats]
    wide = lambda x: jnp.broadcast_to(x, (8, LANES))
    for k in range(0, 32, 4):
        q, s = divmod(k, 8)
        for n, a in enumerate(tiles):
            r = [wide(a[q][s + i : s + i + 1, :]) for i in range(4)]
            cq = [jnp.maximum(wide(a[q][:, k + i : k + i + 1]), -jnp.inf) for i in range(4)]
            m = {(i, j): wide(cq[j][s + i : s + i + 1, :]) for i in range(4) for j in range(i, 4)}
            ia = 1.0 / (m[0, 0] * m[1, 1] - m[0, 1] * m[0, 1])
            x02 = (m[1, 1] * m[0, 2] - m[0, 1] * m[1, 2]) * ia
            x03 = (m[1, 1] * m[0, 3] - m[0, 1] * m[1, 3]) * ia
            x12 = (m[0, 0] * m[1, 2] - m[0, 1] * m[0, 2]) * ia
            x13 = (m[0, 0] * m[1, 3] - m[0, 1] * m[0, 3]) * ia
            s22 = m[2, 2] - m[0, 2] * x02 - m[1, 2] * x12
            s23 = m[2, 3] - m[0, 2] * x03 - m[1, 2] * x13
            s33 = m[3, 3] - m[0, 3] * x03 - m[1, 3] * x13
            ib = 1.0 / (s22 * s33 - s23 * s23)
            t0 = (m[1, 1] * r[0] - m[0, 1] * r[1]) * ia
            t1 = (m[0, 0] * r[1] - m[0, 1] * r[0]) * ia
            z2 = r[2] - x02 * r[0] - x12 * r[1]
            z3 = r[3] - x03 * r[0] - x13 * r[1]
            v2 = (s33 * z2 - s23 * z3) * ib
            v3 = (s22 * z3 - s23 * z2) * ib
            v0 = t0 - x02 * v2 - x03 * v3
            v1 = t1 - x12 * v2 - x13 * v3
            v = (v0, v1, v2, v3)
            got = v0
            for i in (1, 2, 3):
                got = jnp.where(sub8 >= s + i, v[i], got)
            over[n][q] = got if s == 0 else jnp.where(low, got, over[n][q])
            for t in range(q, 4):
                if t == q and s == 4:
                    continue
                c = cq if t == q else [wide(a[t][:, k + i : k + i + 1]) for i in range(4)]
                delta = (c[0] * v0 + c[1] * v1) + (c[2] * v2 + c[3] * v3)
                if t == q:
                    delta = jnp.where(low, delta, 0.0)
                a[t] = a[t] - delta
    u = [jnp.concatenate(a, axis=0) for a in tiles]
    v = [jnp.concatenate(a, axis=0) for a in over]
    return u, v


def finish_factor(u):
    sub8 = iota((8, LANES), 0)
    low = sub8 < 4
    within = sub8 & 3
    wide = lambda x: jnp.broadcast_to(x, (8, LANES))
    out = []
    for t in range(4):
        a = u[8 * t : 8 * t + 8]
        scale = jnp.zeros((8, LANES), F32)
        for i in range(4):
            row = jnp.where(low, wide(a[i : i + 1]), wide(a[4 + i : 5 + i]))
            at = 8 * t + i
            pivot = jnp.where(low, wide(row[:, at : at + 1]), wide(row[:, at + 4 : at + 5]))
            inv = 1.0 / pivot
            scale = jnp.where(within == i, jnp.sqrt(inv), scale)
            if i < 3:
                col = jnp.where(low, wide(a[:, at : at + 1]), wide(a[:, at + 4 : at + 5]))
                a = a - jnp.where(within > i, col * (row * inv), 0.0)
        out.append(a * scale)
    return jnp.concatenate(out, axis=0)


def tn_high(a, b):
    return nn_high(jnp.transpose(a), b)


def setup_kernel(recv_ref, probe_ref, small_ref):
    lane = iota((32, LANES), 1)
    gram = jnp.zeros((32, LANES), F32)
    for i in range(16):
        slab = recv_ref[:, i, :]
        moved = pltpu.roll(slab, (8 * i - 112) % LANES, 1)
        gram = jnp.where((lane >> 3) == i, moved, gram)
    gram = jnp.concatenate([gram[:, :64], gram[:, 64:]], axis=0)
    scaled = probe_ref[0:32]
    half = nn_high(scaled, gram)
    core = lax.dot_general(
        half, scaled, (((1,), (1,)), ((), ())), precision=HIGHEST, preferred_element_type=F32
    )
    eye = (iota((32, 32), 0) == iota((32, 32), 1)).astype(F32)
    zero64 = jnp.zeros((32, 64), F32)
    (u,), _ = eliminate([jnp.concatenate([core, eye, zero64], axis=1)])
    linv = finish_factor(u)[:, 32:64]
    projected = nn_high(linv, half)
    prior = lax.dot_general(
        projected * probe_ref[32:33],
        projected,
        (((1,), (1,)), ((), ())),
        precision=HIGHEST,
        preferred_element_type=F32,
    )
    (u,), (v,) = eliminate([jnp.concatenate([prior, eye, zero64], axis=1)])
    prec = tn_high(v[:, 32:64], u[:, 32:64])
    prec = 0.5 * (prec + jnp.transpose(prec))
    small_ref[...] = jnp.concatenate([linv, prec, zero64], axis=1)


def unfold(x, roll):
    row, lane = iota((16, LANES), 0), iota((16, LANES), 1)
    col = lane & 15
    turned = jnp.transpose(x)
    turned = jnp.concatenate([turned[16 * b : 16 * b + 16] for b in range(8)], axis=1)
    top = jnp.where((lane < 96) & ((lane & 16) == 0) & (row > col), turned, x)
    diag = jnp.zeros((16, LANES), F32)
    for d in range(3):
        diag = jnp.where((lane >> 5) == d, x[:, 102 + d : 103 + d], diag)
    corner = roll(jnp.where(row > col, x, turned), 16, 1)
    corner = jnp.where(row == col, diag, corner)
    low = jnp.where((lane & 16) == 0, roll(turned, LANES - 16, 1), corner)
    low = jnp.where(lane < 96, low, roll(x, LANES - 3, 1))
    both = jnp.concatenate([top, low], axis=0)
    return jnp.where(iota((32, LANES), 1) < 99, both, 0.0)


def solve_kernel(recv_ref, small_ref, fp_ref, mean_hbm, spread_hbm, e_s, x_s, b_s, mean_ref, spread_ref, sems):
    lane = iota((32, LANES), 1)
    linv, prec = small_ref[:, :32], small_ref[:, 32:64]
    cells = fp_ref.shape[1]
    step = 1024
    lt = jnp.transpose(linv)
    zero32 = jnp.zeros((32, 32), F32)
    eye = (iota((32, 32), 0) == iota((32, 32), 1)).astype(F32)
    k3 = jnp.concatenate([prec, prec, prec, zero32], axis=1)
    per_day = jnp.concatenate(
        [
            jnp.concatenate([x if i == j else zero32 for j in range(4)], axis=1)
            for i, x in enumerate((lt, lt, lt, eye))
        ],
        axis=0,
    )
    zero_row = jnp.zeros((1, LANES), F32)
    dcols = []
    for r in range(8):
        x = recv_ref[r, :16, :]
        x_s[:, r * LANES : (r + 1) * LANES] = unfold(x, pltpu.roll)
        for d in range(3):
            column = (x[:, 105 + d : 106 + d], x[:, 108 + d : 109 + d])
            dcols.append(jnp.concatenate(column, axis=0))
    z = nn_high(linv, x_s[...])
    zs = jnp.concatenate([z[:, r * LANES : (r + 1) * LANES] for r in range(8)], axis=0)
    hs = nn_high(zs, per_day)
    first = [recv_ref[b // 3, 16 + b % 3 : 17 + b % 3, :] for b in range(24)]
    first.append(jnp.where(iota((1, LANES), 1) < 32, 1.0, 0.0))
    second = [recv_ref[b // 3, 19 + b % 3 : 20 + b % 3, :] for b in range(24)] + [zero_row]
    dcols.append(jnp.zeros((32, 1), F32))
    for b in range(25):
        nxt = (b + 1) % 25
        e = k3 * first[b] + (k3 * dcols[nxt]) * second[nxt]
        if b < 24:
            h = hs[32 * (b // 3) : 32 * (b // 3) + 32]
            d = b % 3
            mat = h if d == 0 else pltpu.roll(h, LANES - 32 * d, 1)
            vec = h if d == 0 else pltpu.roll(h, LANES - d, 1)
            e = e + jnp.where(lane < 32, mat, jnp.where(lane == 96, vec, 0.0))
        e_s[b] = e
    start = 3 * lax.axis_index("tm")
    nodes = [e_s[lax.rem(start + j, 25)] for j in range(25)]

    plan = [
        {0: [1, 3, 5, 7, 9, 11, 13, 15, 17, 19, 21, 23], 1: [2, 6, 10, 14, 18, 22], 2: [4, 12, 20], 3: [8, 24], 4: [16]},
        {0: [3, 5, 7, 9, 11, 13, 15, 17, 19, 21, 23], 1: [2, 6, 10, 14, 18, 22, 0], 2: [4, 12, 20], 3: [8, 24], 4: [16]},
        {0: [3, 5, 7, 9, 11, 13, 15, 17, 19, 21, 23, 1], 1: [6, 10, 14, 18, 22, 0], 2: [4, 12, 20], 3: [8, 24], 4: [16]},
    ]
    rings = [[(j, j) for j in range(25)] for _ in range(3)]
    values = dict(enumerate(nodes))
    fresh = [25]
    updated = {}

    def renew(key, make):
        if key not in updated:
            values[fresh[0]] = make()
            updated[key] = fresh[0]
            fresh[0] += 1
        return updated[key]

    for level in range(5):
        todo = []
        for target in range(3):
            held = dict(rings[target])
            todo += [held[j] for j in plan[target][level] if held[j] not in todo]
        us, vs = eliminate([values[i] for i in todo])
        prods = {}
        for i, u, v in zip(todo, us, vs):
            prods[i] = nn_high(jnp.transpose(v)[32:96], u)
        for target in range(3):
            ring = rings[target]
            gone = plan[target][level]
            size = len(ring)
            out = []
            for at, (j, i) in enumerate(ring):
                if j in gone:
                    continue
                pj, pi = ring[at - 1]
                nj, ni = ring[(at + 1) % size]
                key = i
                if nj in gone:
                    def as_left(i=i, ni=ni):
                        p = prods[ni][:32]
                        own = jnp.where(lane < 32, pltpu.roll(p, LANES - 32, 1), jnp.where(lane >= 64, p, 0.0))
                        kept = jnp.where((lane < 64) | (lane >= 96), values[i], 0.0)
                        return kept - own

                    i = renew(("l", i, ni), as_left)
                if pj in gone:
                    def as_right(i=i, pi=pi):
                        p = prods[pi][32:]
                        own = jnp.where(
                            lane < 32,
                            pltpu.roll(p, LANES - 64, 1),
                            jnp.where((lane < 64) | (lane >= 96), p, 0.0),
                        )
                        kept = jnp.where((lane < 32) | (lane >= 64), values[i], 0.0)
                        return kept - own

                    i = renew(("r", i, pi), as_right)
                out.append((j, i))
            rings[target] = out
    one, two = halves(linv)
    onto = jnp.concatenate([one, one, two], axis=1).astype(BF16)
    for c in range(0, cells, step):
        basis = jnp.dot(onto, fp_ref[:, c : c + step], preferred_element_type=F32)
        top = basis.astype(BF16)
        b_s[0:32, c : c + step] = top
        b_s[32:64, c : c + step] = (basis - top.astype(F32)).astype(BF16)
        b_s[64:96, c : c + step] = top
    eye_at = jnp.where(lane == iota((32, LANES), 0) + 32, 1.0, 0.0)
    last = []
    for target in range(3):
        (pair,) = rings[target]
        m = values[pair[1]]
        m = m + jnp.where(lane < 32, pltpu.roll(m, LANES - 32, 1) + pltpu.roll(m, LANES - 64, 1), 0.0)
        last.append(jnp.where((lane < 32) | (lane >= 96), m, 0.0) + eye_at)
    us, vs = eliminate(last)
    rows, sums = [], []
    for u, v in zip(us, vs):
        vt = jnp.transpose(v)
        cov = nn_high(vt[32:64], u)[:, 32:64]
        rows.append(cov)
        sums.append(nn_high(vt[96:104], u)[0:1, 32:64])
    lhs = jnp.concatenate(rows + sums + [jnp.zeros((5, 32), F32)], axis=0)
    one, two = halves(lhs)
    lhs = jnp.concatenate([one, one, two], axis=1).astype(BF16)
    copies = []
    for part in range(2):
        half = slice(part * cells // 2, (part + 1) * cells // 2)
        for c in range(half.start, half.stop, step):
            b = b_s[:, c : c + step]
            y = jnp.dot(lhs, b, preferred_element_type=F32)
            wide = b[0:32].astype(F32) + b[32:64].astype(F32)
            for d in range(3):
                spread_ref[d : d + 1, c : c + step] = jnp.sum(
                    y[32 * d : 32 * d + 32] * wide, axis=0, keepdims=True
                )
            mean_ref[:, c : c + step] = y[96:99]
        for k, (ref, hbm) in enumerate(((mean_ref, mean_hbm), (spread_ref, spread_hbm))):
            copies.append(pltpu.make_async_copy(ref.at[:, half], hbm.at[:, half], sems.at[part, k]))
            copies[-1].start()
    for copy in copies:
        copy.wait()


def shape(*dims, dtype=F32):
    return jax.ShapeDtypeStruct(dims, dtype)


def on_chip(*xs):
    return tuple(pltpu.with_memory_space_constraint(x, pltpu.VMEM) for x in xs)


def call(kernel, out, scratch=(), in_specs=None, name=None, out_specs=None):
    extra = {} if in_specs is None else {"in_specs": in_specs}
    if out_specs is not None:
        extra["out_specs"] = out_specs
    return pl.pallas_call(
        kernel, out_shape=out, scratch_shapes=list(scratch), compiler_params=PARAMS, name=name, **extra
    )


VM = pl.BlockSpec(memory_space=pltpu.VMEM)
SM = pl.BlockSpec(memory_space=pltpu.SMEM)
ANY = pl.BlockSpec(memory_space=pl.ANY)


def body(
    background, probe, member_scale, decay, inflation, obs_owner, obs_offset, obs_value, obs_weight
):
    bt = background.T
    probe_t = probe.T
    scale = member_scale.reshape(1, -1)
    owner = obs_owner.transpose(0, 2, 1)
    cells = bt.shape[1]
    send = call(
        bucket_kernel,
        pltpu.VMEM((32, 1, 1280), F32),
        [
            pltpu.VMEM(bt.shape, BF16),
            pltpu.VMEM((3 * 16 * 32, 128), BF16),
            pltpu.SemaphoreType.DMA,
        ],
        in_specs=[VM, VM, VM, VM, ANY],
        name="buckets",
    )(owner, obs_offset, obs_value, obs_weight, bt)
    recv = lax.all_to_all(send, "space", 0, 0, tiled=True)
    ft, fp, scaled_probe, days = call(
        field_kernel,
        (
            pltpu.VMEM((32, cells), F32),
            pltpu.VMEM((96, cells), BF16),
            pltpu.VMEM((40, 64), F32),
            pltpu.VMEM((24, 128), F32),
        ),
        in_specs=[VM, VM, VM, VM, VM, SM],
        name="field",
    )(bt, probe_t, scale, decay, decay.T, inflation)
    recv, ft, fp, scaled_probe, days = on_chip(recv, ft, fp, scaled_probe, days)
    payload = call(
        gram_kernel,
        pltpu.VMEM((32, 16, 128), F32),
        [
            pltpu.VMEM((3, 64, 128), F32),
            pltpu.VMEM((3, 64, 128), F32),
            pltpu.VMEM((16, 128), F32),
        ],
        name="grams",
    )(recv, ft, fp)
    recv_2 = lax.all_to_all(payload, "space", 0, 0, tiled=True)
    (recv_2,) = on_chip(recv_2)
    both = call(total_kernel, pltpu.VMEM((8, 24, 128), F32), name="totals")(recv_2, days)
    recv_3 = lax.all_to_all(both, "tm", 0, 0, tiled=True)
    (recv_3,) = on_chip(recv_3)
    small = call(setup_kernel, pltpu.VMEM((32, 128), F32), name="setup")(recv_2, scaled_probe)
    (small,) = on_chip(small)
    mean, spread = call(
        solve_kernel,
        (shape(3, cells), shape(3, cells)),
        [
            pltpu.VMEM((25, 32, 128), F32),
            pltpu.VMEM((32, 1024), F32),
            pltpu.VMEM((96, cells), BF16),
            pltpu.VMEM((3, cells), F32),
            pltpu.VMEM((3, cells), F32),
            pltpu.SemaphoreType.DMA((2, 2)),
        ],
        in_specs=[VM, VM, VM],
        out_specs=(ANY, ANY),
        name="solve",
    )(recv_3, small, fp)
    return mean, spread


def solution(mesh):
    return jax.shard_map(
        body,
        mesh=mesh,
        in_specs=(
            P("space", None),
            P(),
            P(),
            P("tm", None),
            P("tm"),
            P("tm", "space", None),
            P("tm", "space"),
            P("tm", "space"),
            P("tm", "space"),
        ),
        out_specs=(P("tm", "space"), P("tm", "space")),
        check_vma=False,
    )
```
